256 devices in a mesh: shot: 16 (over z, y_hi), grid: 16 (over x, y_lo, core).
Axes of the slice: x: 4, y: 4 (y_hi: 2, y_lo: 2; y = y_hi * 2 + y_lo), z: 8, core: 2. Of those that a mesh axis runs over, the one named last changes fastest.
Arguments:
- residuals: bfloat16 [4096, 4, 2048], P('shot', None, 'grid'), may hold values from -6 to 6
- encoding: bfloat16 [16, 4096], P(None, 'shot'), may hold values from -0.125 to 0.125
- receiver_cells: int32 [3, 2048], replicated, may hold values from 0 to 255, as said below
- velocity_term: float32 [256, 128, 256], P('grid'), may hold values from 0.02 to 0.18
- field_before: float32 [16, 256, 128, 256], P('shot', 'grid'), may hold values from -6 to 6
- field_start: float32 [16, 256, 128, 256], P('shot', 'grid'), may hold values from -6 to 6
Outputs:
- field_last: float32 [16, 256, 128, 256], P('shot', 'grid')
- field_end: float32 [16, 256, 128, 256], P('shot', 'grid')
The draws below stay inside these ranges and needn't reach their ends.
Inputs may be any that keep to these rules, and one draw needn't show every extreme that they name: `receiver_cells`: row 0 holds first-dimension cells below 256, row 1 second-dimension cells below 128, row 2 third-dimension cells below 8.
All inputs are finite; a program needn't handle non-finite values.
Results may differ from the reference program's by a relative error of at most 0.0003.
Values sent between devices are 32-bit elements; how exact they have to be, the bound alone decides.
A program may use at most 128 MiB of HBM per device.

```python
import math
import jax
import jax.numpy as jnp
from jax import lax

NY = 128
NZ = 256
STEPS = 4
SUPERSHOTS = 16
SHOTS = 4096
RECEIVERS = 2048
NX = 256


def draw_receiver_cells(key, part):
    first_key, second_key, third_key = jax.random.split(jax.random.fold_in(key, 17), 3)
    first = jax.random.randint(first_key, (RECEIVERS,), 0, NX)
    second = jax.random.randint(second_key, (RECEIVERS,), 0, NY)
    third = jax.random.randint(third_key, (RECEIVERS,), 0, 8)
    return jnp.stack([first, second, third]).astype(jnp.int32)


def spiked(result, stream_key, source, target, parts, factor):
    def block_of(dim):
        return (jnp.arange(result.shape[dim]) // (result.shape[dim] // parts)).reshape((-1,) + (1,) * (result.ndim - 1 - dim))

    first = jax.random.permutation(stream_key, parts)[block_of(target)]
    far = (block_of(target) + parts // 2) % parts
    return jnp.where((block_of(source) == first) | (block_of(source) == far), factor * result, result)


def block_levels(own_key, shape, shards, low, high):
    factor_of = 1.0
    for axis_at, blocks in shards:
        steps = jax.random.uniform(jax.random.fold_in(jax.random.fold_in(own_key, 6), axis_at), (blocks,), jnp.float32, low / len(shards), high / len(shards))
        factor_of = factor_of * jnp.repeat(jnp.exp(steps), shape[axis_at] // blocks).reshape((-1,) + (1,) * (len(shape) - 1 - axis_at))
    return factor_of


def bell_draw(rng, shape, scale, limit, cuts=(), held_as=jnp.bfloat16):
    values = scale * jax.random.normal(rng, shape, jnp.float32)
    if cuts:
        values = values * block_levels(rng, shape, cuts, -0.22, 0.18)
    return jnp.clip(values, -limit, limit).astype(held_as)


def bell_draw_with(stream_key, shape, spread, bound, pieces, heavy, dtype=jnp.bfloat16):
    entries = spread * jax.random.normal(stream_key, shape, jnp.float32)
    if pieces:
        entries = entries * block_levels(stream_key, shape, pieces, -0.22, 0.18)
    return jnp.clip(spiked(entries, jax.random.fold_in(stream_key, 3), *heavy), -bound, bound).astype(dtype)


def setup_inputs(seed: int = 0) -> dict:
    key_of = jax.random.split(jax.random.key(seed), 7)
    return {
        "residuals": bell_draw(key_of[0], (SHOTS, STEPS, RECEIVERS), 1.0, 6.0, ((0, 16), (2, 16))),
        "encoding": bell_draw_with(key_of[1], (SUPERSHOTS, SHOTS), SHOTS ** -0.5, 0.125, ((1, 16),), (1, 0, 16, 2.0)),
        "receiver_cells": draw_receiver_cells(jax.random.fold_in(key_of[6], 71), 0),
        "velocity_term": jnp.clip(jnp.exp(math.log(0.18) - 2.1972246 * jax.random.uniform(key_of[3], (NX, NY, NZ), jnp.float32) ** block_levels(key_of[3], (NX, NY, NZ), ((0, 16),), -0.2, 0.2)), 0.02, 0.18),
        "field_before": bell_draw(key_of[4], (SUPERSHOTS, NX, NY, NZ), 1.0, 6.0, ((0, 16), (1, 16)), jnp.float32),
        "field_start": bell_draw(key_of[5], (SUPERSHOTS, NX, NY, NZ), 1.0, 6.0, ((0, 16), (1, 16)), jnp.float32),
    }


coeffs = (-205.0 / 72.0, 8.0 / 5.0, -1.0 / 5.0, 8.0 / 315.0, -1.0 / 560.0)


def laplace(extended):
    width = extended.shape[0] - 8
    center = extended[4:4 + width]
    padded = jnp.pad(center, ((0, 0), (4, 4), (4, 4)))
    rows = center.shape[1]
    depth = center.shape[2]
    total = 3.0 * coeffs[0] * center
    for shift in range(1, 5):
        along_x = extended[4 + shift:4 + shift + width] + extended[4 - shift:4 - shift + width]
        along_y = padded[:, 4 + shift:4 + shift + rows, 4:4 + depth] + padded[:, 4 - shift:4 - shift + rows, 4:4 + depth]
        along_z = padded[:, 4:4 + rows, 4 + shift:4 + shift + depth] + padded[:, 4:4 + rows, 4 - shift:4 - shift + depth]
        total = total + coeffs[shift] * (along_x + along_y + along_z)
    return total


def inject(field, start_x, cells, values):
    width, rows, depth = field.shape
    local_x = cells[0] - start_x
    inside = (local_x >= 0) & (local_x < width)
    flat = (local_x * rows + cells[1]) * depth + cells[2]
    flat = jnp.where(inside, flat, width * rows * depth).astype(jnp.int32)
    return field.reshape(-1).at[flat].add(values, mode="drop").reshape(field.shape)


def reference(residuals, encoding, receiver_cells, velocity_term, field_before, field_start):
    encoded = jnp.dot(encoding, residuals.reshape(SHOTS, STEPS * RECEIVERS), preferred_element_type=jnp.float32)
    encoded = encoded.reshape(SUPERSHOTS, STEPS, RECEIVERS)

    def propagate(items):
        previous, current, traces = items
        for step in range(STEPS):
            extended = jnp.pad(current, ((4, 4), (0, 0), (0, 0)))
            advanced = 2.0 * current - previous + velocity_term * laplace(extended)
            advanced = inject(advanced, 0, receiver_cells, traces[STEPS - 1 - step])
            previous, current = current, advanced
        return previous, current

    field_last, field_end = lax.map(propagate, (field_before, field_start, encoded))
    return field_last, field_end
```

```python
import functools

import jax
import jax.numpy as jnp
from jax import lax
from jax.experimental import pallas as pl
from jax.experimental.pallas import tpu as pltpu
from jax.sharding import PartitionSpec as P

C0, C1, C2, C3, C4 = (-205.0 / 72.0, 8.0 / 5.0, -1.0 / 5.0, 8.0 / 315.0, -1.0 / 560.0)
SCALE = 5040.0
BAND = (8064.0, -1008.0, 128.0, -9.0)
MESH = pl.DeviceIdType.MESH
F32 = jnp.float32
BF16 = jnp.bfloat16


def band_of(distance):
    value = jnp.zeros(distance.shape, F32)
    for j, weight in enumerate(BAND, 1):
        value = jnp.where(distance == j, weight, value)
    return value.astype(BF16)


def iota(shape, dim):
    return lax.broadcasted_iota(jnp.int32, shape, dim)


def split(value):
    high = value.astype(BF16)
    return high, (value - high.astype(F32)).astype(BF16)


def dot(a, b):
    return jnp.dot(a, b, preferred_element_type=F32)


def kernel(
    n_grid, n_shot, res_hbm, enc_hbm, cells_hbm, vt_hbm, before_hbm, start_hbm, last_hbm, end_hbm,
    fa, fb, vt, halo, zmat, ymat, res, enc, cells, part, other, shots, traces, oy, oxz, inj,
    load_sem, out_sem, send_sem, recv_sem, pair_sem, shot_send, shot_recv, grid_send, grid_recv, ready,
):
    g = lax.axis_index("grid")
    s = lax.axis_index("shot")
    width, rows, depth = vt.shape
    half = depth // 2
    even = lax.rem(g, 2) == 0
    odd = lax.rem(g, 2) == 1
    has = (g > 0, g < n_grid - 1)
    near = (jnp.maximum(g - 1, 0), jnp.minimum(g + 1, n_grid - 1))
    pair = g // 2

    loads = [
        pltpu.make_async_copy(src, dst, load_sem.at[i])
        for i, (src, dst) in enumerate((
            (res_hbm, res),
            (enc_hbm, enc),
            (start_hbm.at[0], fb.at[pl.ds(4, width)]),
            (before_hbm.at[0], fa.at[pl.ds(4, width)]),
            (vt_hbm, vt),
            (cells_hbm, cells),
        ))
    ]
    for load in loads:
        load.start()

    barrier = pltpu.get_barrier_semaphore()

    def greet(**device):
        pl.semaphore_signal(barrier, inc=1, device_id=device, device_id_type=MESH)

    @pl.when(even)
    def _():
        greet(grid=near[1])

        @pl.when(has[0])
        def _():
            greet(grid=near[0])

        for k in range(1, n_shot):
            greet(shot=lax.rem(s + k, n_shot))
        for k in range(2, n_grid, 2):
            greet(grid=lax.rem(g + k, n_grid))

    @pl.when(odd)
    def _():
        for k in range(1, n_grid, 2):
            greet(grid=lax.rem(g + k, n_grid))

    zmat[...] = band_of(jnp.abs(iota((depth, depth), 0) - iota((depth, depth), 1)))
    ymat[...] = band_of(jnp.abs(iota((rows, 2 * rows), 0) - lax.rem(iota((rows, 2 * rows), 1), rows)))
    for f in (fa, fb):
        for p in (0, width + 4):
            f[pl.ds(p, 4)] = jnp.zeros((4, rows, depth), F32)

    def halo_copy(n, side, h, src):
        lanes = pl.ds(h * half, half)
        return pltpu.make_async_remote_copy(
            src_ref=src.at[:, :, lanes],
            dst_ref=halo.at[n, 1 - side, :, :, lanes],
            send_sem=send_sem.at[n, side, h],
            recv_sem=recv_sem.at[n, 1 - side, h],
            device_id={"grid": near[side]},
            device_id_type=MESH,
        )

    def edge_of(n, side):
        if n == 0:
            return start_hbm.at[0, pl.ds(0 if side == 0 else width - 4, 4)]
        f = fb if n % 2 == 0 else fa
        return f.at[pl.ds(4 if side == 0 else width, 4)]

    def send_halo(n, side, h):
        @pl.when(has[side])
        def _():
            halo_copy(n, side, h, edge_of(n, side)).start()

    def wait_sent(n):
        for side in (0, 1):
            @pl.when(has[side])
            def _():
                for h in (1, 0):
                    halo_copy(n, side, h, edge_of(n, side)).wait_send()

    def pair_copy(target):
        return pltpu.make_async_remote_copy(
            src_ref=part, dst_ref=other, send_sem=pair_sem.at[0], recv_sem=pair_sem.at[1],
            device_id={"grid": target}, device_id_type=MESH,
        )

    @pl.when(odd)
    def _():
        pl.semaphore_wait(barrier, jnp.where(has[1], 2, 1))
        for side in (0, 1):
            @pl.when(has[side])
            def _():
                pl.semaphore_signal(ready.at[1 - side], inc=1, device_id={"grid": near[side]}, device_id_type=MESH)

    for side in (1, 0):
        @pl.when(even & has[side])
        def _():
            pl.semaphore_wait(ready.at[side], 1)
    for h in (1, 0):
        for side in (0, 1):
            send_halo(0, side, h)

    loads[0].wait()
    loads[1].wait()
    shot_rows, samples = res.shape[0] // 4, 4
    core = lax.rem(g, 2)
    r = iota((8 * n_shot, n_shot), 0)
    pick = jnp.where(r // 8 == iota((8 * n_shot, n_shot), 1), 1.0, 0.0).astype(BF16)
    spread = jnp.where(
        iota((shot_rows, 4 * shot_rows), 0) == iota((shot_rows, 4 * shot_rows), 1) // 4, 1.0, 0.0
    ).astype(BF16)
    weights = dot(dot(pick, enc[...]).astype(BF16), spread)
    wide = (8 * n_shot, 4 * shot_rows)
    weights = jnp.where(lax.rem(iota(wide, 0), 8) - 4 * core == lax.rem(iota(wide, 1), 4), weights, 0.0)
    part[...] = dot(weights.astype(BF16), res[...]).reshape(n_shot, 8, 128)

    @pl.when(odd)
    def _():
        pair_copy(near[0]).start()

    for load in loads[2:]:
        load.wait()

    n_rec = cells.shape[1]
    oy[...] = jnp.where(iota((rows, n_rec), 0) == cells[1:2, :], 1.0, 0.0).astype(BF16)
    spot = (cells[0:1, :] - g * width) * 8 + cells[2:3, :]
    oxz[...] = jnp.where(iota((8 * width, n_rec), 0) == spot, 1.0, 0.0).astype(BF16)

    def own_part(n):
        cur, nxt = (fb, fa) if n % 2 == 0 else (fa, fb)

        def plane(x, carry):
            u = cur[x + 4]
            high, low = split(u)
            across = dot(jnp.concatenate([high, low], axis=1), jnp.concatenate([zmat[...], zmat[...]], axis=0))
            across = across + dot(ymat[...], jnp.concatenate([high, low], axis=0))
            total = (3.0 * C0) * u + across * (1.0 / SCALE)
            for j, weight in enumerate((C1, C2, C3, C4), 1):
                total = total + weight * (cur[x + 4 + j] + cur[x + 4 - j])
            nxt[x + 4] = 2.0 * u - nxt[x + 4] + vt[x] * total
            return carry

        lax.fori_loop(0, width, plane, 0)

    def add_halo(n, side, h):
        nxt = fa if n % 2 == 0 else fb
        lanes = pl.ds(h * half, half)

        @pl.when(has[side])
        def _():
            halo_copy(n, 1 - side, h, edge_of(n, 1 - side)).wait_recv()
            layer = [halo[n, side, 4 - d if side == 0 else d - 1, :, lanes] for d in (1, 2, 3, 4)]
            for i in range(4):
                x = i if side == 0 else width - 1 - i
                total = C4 * layer[3 - i]
                for j, weight in ((1, C1), (2, C2), (3, C3)):
                    if j > i:
                        total = total + weight * layer[j - i - 1]
                nxt[x + 4, :, lanes] = nxt[x + 4, :, lanes] + vt[x, :, lanes] * total

    def inject(n, planes):
        nxt = fa if n % 2 == 0 else fb
        lane = iota((rows, half), 1)
        values = inj[3 - n]
        for x in planes:
            moved = values if x == 0 else pltpu.roll(values, half - 8 * x, 1)
            nxt[x + 4, :, pl.ds(0, half)] = nxt[x + 4, :, pl.ds(0, half)] + jnp.where(lane < 8, moved, 0.0)

    edges = list(range(4)) + list(range(width - 4, width))
    inner = list(range(4, width - 4))

    own_part(0)

    def shot_copy(k):
        return pltpu.make_async_remote_copy(
            src_ref=part.at[k], dst_ref=shots.at[s], send_sem=shot_send.at[k], recv_sem=shot_recv.at[s],
            device_id={"shot": k}, device_id_type=MESH,
        )

    def shot_arrival(k):
        return pltpu.make_async_remote_copy(
            src_ref=part.at[k], dst_ref=shots.at[k], send_sem=shot_send.at[k], recv_sem=shot_recv.at[k],
            device_id={"shot": k}, device_id_type=MESH,
        )

    def grid_copy(target):
        return pltpu.make_async_remote_copy(
            src_ref=traces.at[pair], dst_ref=traces.at[pair], send_sem=grid_send.at[target], recv_sem=grid_recv.at[pair],
            device_id={"grid": target}, device_id_type=MESH,
        )

    def grid_arrival(e):
        return pltpu.make_async_remote_copy(
            src_ref=traces.at[e], dst_ref=traces.at[e], send_sem=grid_send.at[e], recv_sem=grid_recv.at[e],
            device_id={"grid": 2 * e}, device_id_type=MESH,
        )

    @pl.when(even)
    def _():
        pair_copy(near[1]).wait_recv()
        part[...] = part[...] + other[...]
        shots[s] = part[s]
        pl.semaphore_wait(barrier, n_shot - 1 + n_grid - 1)
        for i in range(1, n_shot):
            shot_copy(lax.rem(s + i, n_shot)).start()

    for side in (0, 1):
        add_halo(0, side, 1)
        send_halo(1, side, 1)

    @pl.when(even)
    def _():
        for i in range(1, n_shot):
            shot_arrival(lax.rem(s + i, n_shot)).wait_recv()
        traces[pair] = jnp.sum(shots[...], axis=0)
        for i in range(1, n_grid):
            grid_copy(lax.rem(g + i, n_grid)).start()

    for i in range(n_grid // 2):
        @pl.when(jnp.logical_not(even & (pair == i)))
        def _():
            grid_arrival(i).wait_recv()

    for t in range(4):
        row = jnp.concatenate([traces[i // 2, pl.ds(4 * (i % 2) + t, 1), :] for i in range(n_grid)], axis=1)
        total = jnp.zeros((rows, 8 * width), F32)
        for piece in split(row):
            scaled = oy[...] * jnp.broadcast_to(piece, oy.shape)
            total = total + lax.dot_general(scaled, oxz[...], (((1,), (1,)), ((), ())), preferred_element_type=F32)
        inj[t] = total

    inject(0, edges)
    for side in (0, 1):
        add_halo(0, side, 0)
        send_halo(1, side, 0)
    inject(0, inner)

    outs = []

    def put(f, out, at, length, lanes, sem):
        copy = pltpu.make_async_copy(
            f.at[pl.ds(at + 4, length), :, lanes], out.at[0, pl.ds(at, length), :, lanes], out_sem.at[sem]
        )
        copy.start()
        outs.append(copy)

    for n in (1, 2, 3):
        wait_sent(n - 1)
        own_part(n)
        inject(n, edges)
        if n == 3:
            inject(n, inner)
            put(fb, end_hbm, 4, width - 8, pl.ds(0, depth), 1)
        for h in (1, 0):
            for side in (0, 1):
                add_halo(n, side, h)
                if n < 3:
                    send_halo(n + 1, side, h)
                else:
                    put(fb, end_hbm, 0 if side == 0 else width - 4, 4, pl.ds(h * half, half), 2 + 2 * h + side)
        if n < 3:
            inject(n, inner)
        if n == 2:
            put(fa, last_hbm, 0, width, pl.ds(0, depth), 0)

    wait_sent(3)
    for copy in outs:
        copy.wait()

    @pl.when(odd)
    def _():
        pair_copy(near[0]).wait_send()

    @pl.when(even)
    def _():
        for i in range(1, n_shot):
            shot_copy(lax.rem(s + i, n_shot)).wait_send()
        for i in range(1, n_grid):
            grid_copy(lax.rem(g + i, n_grid)).wait_send()


def local(n_grid, n_shot, residuals, encoding, receiver_cells, velocity_term, field_before, field_start):
    shot_rows, samples, local_receivers = residuals.shape
    width, rows, depth = velocity_term.shape
    flat = residuals.reshape(shot_rows * samples, local_receivers)
    n_rec = receiver_cells.shape[1]
    any_space = pl.BlockSpec(memory_space=pl.ANY)
    dma = pltpu.SemaphoreType.DMA
    field = jax.ShapeDtypeStruct(field_start.shape, F32)
    return pl.pallas_call(
        functools.partial(kernel, n_grid, n_shot),
        out_shape=(field, field),
        in_specs=[pl.BlockSpec(memory_space=pltpu.HBM)] * 6,
        out_specs=(any_space, any_space),
        scratch_shapes=[
            pltpu.VMEM((width + 8, rows, depth), F32),
            pltpu.VMEM((width + 8, rows, depth), F32),
            pltpu.VMEM((width, rows, depth), F32),
            pltpu.VMEM((4, 2, 4, rows, depth), F32),
            pltpu.VMEM((depth, depth), BF16),
            pltpu.VMEM((rows, 2 * rows), BF16),
            pltpu.VMEM(flat.shape, BF16),
            pltpu.VMEM(encoding.shape, BF16),
            pltpu.VMEM(receiver_cells.shape, jnp.int32),
            pltpu.VMEM((n_shot, 8, local_receivers), F32),
            pltpu.VMEM((n_shot, 8, local_receivers), F32),
            pltpu.VMEM((n_shot, 8, local_receivers), F32),
            pltpu.VMEM((n_grid // 2, 8, local_receivers), F32),
            pltpu.VMEM((rows, n_rec), BF16),
            pltpu.VMEM((8 * width, n_rec), BF16),
            pltpu.VMEM((4, rows, 8 * width), F32),
            dma((6,)),
            dma((6,)),
            dma((4, 2, 2)),
            dma((4, 2, 2)),
            dma((2,)),
            dma((n_shot,)),
            dma((n_shot,)),
            dma((n_grid,)),
            dma((n_grid // 2,)),
            pltpu.SemaphoreType.REGULAR((2,)),
        ],
        compiler_params=pltpu.CompilerParams(
            collective_id=0, has_side_effects=True, vmem_limit_bytes=48 * 1024 * 1024
        ),
        name="window",
    )(flat, encoding, receiver_cells, velocity_term, field_before, field_start)


def solution(mesh):
    return jax.shard_map(
        functools.partial(local, mesh.shape["grid"], mesh.shape["shot"]),
        mesh=mesh,
        in_specs=(
            P("shot", None, "grid"),
            P(None, "shot"),
            P(),
            P("grid", None, None),
            P("shot", "grid", None, None),
            P("shot", "grid", None, None),
        ),
        out_specs=(P("shot", "grid", None, None), P("shot", "grid", None, None)),
        check_vma=False,
    )
```

```python
import functools

import jax
import jax.numpy as jnp
from jax import lax
from jax.experimental import pallas as pl
from jax.experimental.pallas import tpu as pltpu
from jax.sharding import PartitionSpec as P

C0, C1, C2, C3, C4 = (-205.0 / 72.0, 8.0 / 5.0, -1.0 / 5.0, 8.0 / 315.0, -1.0 / 560.0)
SCALE = 5040.0
BAND = (8064.0, -1008.0, 128.0, -9.0)
MESH = pl.DeviceIdType.MESH
F32 = jnp.float32
BF16 = jnp.bfloat16


def band_of(distance):
    value = jnp.zeros(distance.shape, F32)
    for j, weight in enumerate(BAND, 1):
        value = jnp.where(distance == j, weight, value)
    return value.astype(BF16)


def iota(shape, dim):
    return lax.broadcasted_iota(jnp.int32, shape, dim)


def split(value):
    high = value.astype(BF16)
    return high, (value - high.astype(F32)).astype(BF16)


def dot(a, b):
    return jnp.dot(a, b, preferred_element_type=F32)


def kernel(
    n_grid, n_shot, res_hbm, enc_hbm, cells_hbm, vt_hbm, before_hbm, start_hbm, fa, fb,
    vt, halo, stage, zmat, ymat, res, enc, cells, part, other, full, shots, traces, oy, oxz, inj,
    load_sem, send_sem, recv_sem, pair_sem, block_send, block_recv, shot_send, shot_recv, row_send, row_recv, ready,
):
    g = lax.axis_index("grid")
    s = lax.axis_index("shot")
    width, rows, depth = vt.shape
    half = depth // 2
    even = lax.rem(g, 2) == 0
    odd = lax.rem(g, 2) == 1
    has = (g > 0, g < n_grid - 1)
    near = (jnp.maximum(g - 1, 0), jnp.minimum(g + 1, n_grid - 1))
    place = lax.rem(g, 4)
    row = g // 4
    n_rows = n_grid // 4
    flipped = g + jnp.where(place < 2, 2, -2)

    def mate(k):
        return {"grid": jnp.where(lax.rem(k, 2) == lax.rem(s, 2), g, flipped), "shot": k}

    loads = [
        pltpu.make_async_copy(src, dst, load_sem.at[i])
        for i, (src, dst) in enumerate((
            (res_hbm, res),
            (enc_hbm, enc),
            (start_hbm.at[0], fb.at[pl.ds(4, width)]),
            (before_hbm.at[0], fa.at[pl.ds(4, width)]),
            (vt_hbm, vt),
            (cells_hbm, cells),
        ))
    ]
    for load in loads:
        load.start()

    barrier = pltpu.get_barrier_semaphore()

    def greet(**device):
        pl.semaphore_signal(barrier, inc=1, device_id=device, device_id_type=MESH)

    @pl.when(even)
    def _():
        greet(grid=near[1])

        @pl.when(has[0])
        def _():
            greet(grid=near[0])

        for i in range(1, n_shot):
            greet(**mate(lax.rem(s + i, n_shot)))
        for i in range(1, n_rows):
            greet(grid=lax.rem(g + 4 * i, n_grid))

    @pl.when(odd)
    def _():
        for i in range(n_rows):
            greet(grid=lax.rem(g - 1 + 4 * i, n_grid))

    zmat[...] = band_of(jnp.abs(iota((depth, depth), 0) - iota((depth, depth), 1)))
    ymat[...] = band_of(jnp.abs(iota((rows, 2 * rows), 0) - lax.rem(iota((rows, 2 * rows), 1), rows)))
    for f in (fa, fb):
        for p in (0, width + 4):
            f[pl.ds(p, 4)] = jnp.zeros((4, rows, depth), F32)

    def halo_copy(n, side, h, src):
        lanes = pl.ds(h * half, half)
        return pltpu.make_async_remote_copy(
            src_ref=stage.at[side] if (n, h) == (1, 0) else src.at[:, :, lanes],
            dst_ref=halo.at[n, 1 - side, :, :, lanes],
            send_sem=send_sem.at[n, side, h],
            recv_sem=recv_sem.at[n, 1 - side, h],
            device_id={"grid": near[side]},
            device_id_type=MESH,
        )

    def edge_of(n, side):
        if n == 0:
            return start_hbm.at[0, pl.ds(0 if side == 0 else width - 4, 4)]
        f = fb if n % 2 == 0 else fa
        return f.at[pl.ds(4 if side == 0 else width, 4)]

    def send_halo(n, side, h):
        @pl.when(has[side])
        def _():
            halo_copy(n, side, h, edge_of(n, side)).start()

    def wait_sent(n):
        for side in (0, 1):
            @pl.when(has[side])
            def _():
                for h in (1, 0):
                    halo_copy(n, side, h, edge_of(n, side)).wait_send()

    def pair_copy(target):
        return pltpu.make_async_remote_copy(
            src_ref=part, dst_ref=other, send_sem=pair_sem.at[0], recv_sem=pair_sem.at[1],
            device_id={"grid": target}, device_id_type=MESH,
        )

    def block_copy(y, sem, target):
        rows_of = full.at[:, pl.ds(8 * y, 8)]
        return pltpu.make_async_remote_copy(
            src_ref=rows_of, dst_ref=rows_of, send_sem=block_send.at[sem], recv_sem=block_recv.at[y],
            device_id={"grid": target}, device_id_type=MESH,
        )

    loads[0].wait()
    loads[1].wait()
    shot_rows, samples = res.shape[0] // 4, 4
    core = lax.rem(g, 2)
    r = iota((8 * n_shot, n_shot), 0)
    pick = jnp.where(r // 8 == iota((8 * n_shot, n_shot), 1), 1.0, 0.0).astype(BF16)
    spread = jnp.where(
        iota((shot_rows, 4 * shot_rows), 0) == iota((shot_rows, 4 * shot_rows), 1) // 4, 1.0, 0.0
    ).astype(BF16)
    weights = dot(dot(pick, enc[...]).astype(BF16), spread)
    wide = (8 * n_shot, 4 * shot_rows)
    weights = jnp.where(lax.rem(iota(wide, 0), 8) - 4 * core == lax.rem(iota(wide, 1), 4), weights, 0.0)
    part[...] = dot(weights.astype(BF16), res[...]).reshape(n_shot, 8, 128)

    @pl.when(odd)
    def _():
        pl.semaphore_wait(barrier, jnp.where(has[1], 2, 1))
        for side in (0, 1):
            @pl.when(has[side])
            def _():
                pl.semaphore_signal(ready.at[1 - side], inc=1, device_id={"grid": near[side]}, device_id_type=MESH)

    for side in (1, 0):
        @pl.when(even & has[side])
        def _():
            pl.semaphore_wait(ready.at[side], 1)
    @pl.when(place == 0)
    def _():
        pair_copy(near[1]).start()

    @pl.when(place == 3)
    def _():
        pair_copy(near[0]).start()

    over_y = (place == 2, place == 1)
    for h in (1, 0):
        for side in (0, 1):
            @pl.when(jnp.logical_not(over_y[side]))
            def _():
                send_halo(0, side, h)

    @pl.when(place == 1)
    def _():
        pair_copy(near[0]).wait_recv()
        full[:, pl.ds(0, 8)] = part[...] + other[...]
        block_copy(0, 0, near[1]).start()
        block_copy(0, 1, near[0]).start()

    @pl.when(place == 2)
    def _():
        pair_copy(near[1]).wait_recv()
        full[:, pl.ds(8, 8)] = part[...] + other[...]
        block_copy(1, 0, near[0]).start()

    for h in (1, 0):
        for side in (0, 1):
            @pl.when(over_y[side])
            def _():
                send_halo(0, side, h)

    for load in loads[2:]:
        load.wait()

    n_rec = cells.shape[1]
    oy[...] = jnp.where(iota((rows, n_rec), 0) == cells[1:2, :], 1.0, 0.0).astype(BF16)
    spot = (cells[0:1, :] - g * width + 8) * 8 + cells[2:3, :]
    oxz[...] = jnp.where(iota(oxz.shape, 0) == spot, 1.0, 0.0).astype(BF16)

    def own_part(n, lanes=pl.ds(0, depth)):
        cur, nxt = (fb, fa) if n % 2 == 0 else (fa, fb)

        def plane(x, carry):
            high, low = split(cur[x + 4])
            along = zmat[:, lanes]
            across = dot(jnp.concatenate([high, low], axis=1), jnp.concatenate([along, along], axis=0))
            at = slice(lanes.start, lanes.start + lanes.size)
            across = across + dot(ymat[...], jnp.concatenate([high[:, at], low[:, at]], axis=0))
            u = cur[x + 4, :, lanes]
            total = (3.0 * C0) * u + across * (1.0 / SCALE)
            for j, weight in enumerate((C1, C2, C3, C4), 1):
                total = total + weight * (cur[x + 4 + j, :, lanes] + cur[x + 4 - j, :, lanes])
            nxt[x + 4, :, lanes] = 2.0 * u - nxt[x + 4, :, lanes] + vt[x, :, lanes] * total
            return carry

        lax.fori_loop(0, width, plane, 0)

    def add_halo(n, side, h):
        nxt = fa if n % 2 == 0 else fb
        lanes = pl.ds(h * half, half)

        @pl.when(has[side])
        def _():
            halo_copy(n, 1 - side, h, edge_of(n, 1 - side)).wait_recv()
            if (n, h) == (1, 0):
                for p in range(4):
                    x = p - 4 if side == 0 else width + p
                    halo[n, side, p, :, lanes] = halo[n, side, p, :, lanes] + traces_at(0, x)
            layer = [halo[n, side, 4 - d if side == 0 else d - 1, :, lanes] for d in (1, 2, 3, 4)]
            for i in range(4):
                x = i if side == 0 else width - 1 - i
                total = C4 * layer[3 - i]
                for j, weight in ((1, C1), (2, C2), (3, C3)):
                    if j > i:
                        total = total + weight * layer[j - i - 1]
                value = nxt[x + 4, :, lanes] + vt[x, :, lanes] * total
                nxt[x + 4, :, lanes] = value
                if (n, h) == (0, 0):
                    stage[side, i if side == 0 else 3 - i] = value

    def traces_at(n, x):
        tile, lane = divmod(8 * (x + 8), half)
        values = inj[3 - n, :, pl.ds(tile * half, half)]
        moved = values if lane == 0 else pltpu.roll(values, half - lane, 1)
        return jnp.where(iota((rows, half), 1) < 8, moved, 0.0)

    def inject(n, planes):
        nxt = fa if n % 2 == 0 else fb
        for x in planes:
            nxt[x + 4, :, pl.ds(0, half)] = nxt[x + 4, :, pl.ds(0, half)] + traces_at(n, x)

    edges = list(range(4)) + list(range(width - 4, width))
    inner = list(range(4, width - 4))

    own_part(0)

    def shot_copy(k):
        return pltpu.make_async_remote_copy(
            src_ref=full.at[k], dst_ref=shots.at[s], send_sem=shot_send.at[k], recv_sem=shot_recv.at[s],
            device_id=mate(k), device_id_type=MESH,
        )

    def shot_arrival(k):
        return pltpu.make_async_remote_copy(
            src_ref=full.at[k], dst_ref=shots.at[k], send_sem=shot_send.at[k], recv_sem=shot_recv.at[k],
            device_id=mate(k), device_id_type=MESH,
        )

    def row_copy(i, core):
        return pltpu.make_async_remote_copy(
            src_ref=traces.at[row], dst_ref=traces.at[row], send_sem=row_send.at[i, core], recv_sem=row_recv.at[row],
            device_id={"grid": lax.rem(g + 4 * i + core, n_grid)}, device_id_type=MESH,
        )

    def row_arrival(i):
        return pltpu.make_async_remote_copy(
            src_ref=traces.at[i], dst_ref=traces.at[i], send_sem=row_send.at[0, 0], recv_sem=row_recv.at[i],
            device_id={"grid": near[0]}, device_id_type=MESH,
        )

    row_targets = [(i, core) for i in range(n_rows) for core in (0, 1) if i or core]

    @pl.when(place == 1)
    def _():
        block_copy(1, 2, near[1]).wait_recv()
        block_copy(1, 2, near[0]).start()

    @pl.when(place == 0)
    def _():
        block_copy(0, 0, near[1]).wait_recv()
        block_copy(1, 0, near[1]).wait_recv()

    @pl.when(place == 2)
    def _():
        block_copy(0, 0, near[0]).wait_recv()

    @pl.when(even)
    def _():
        shots[s] = full[s]
        pl.semaphore_wait(barrier, n_shot - 1 + 2 * n_rows - 1)
        for i in range(1, n_shot):
            shot_copy(lax.rem(s + i, n_shot)).start()

    for side in (0, 1):
        add_halo(0, side, 1)
        send_halo(1, side, 1)

    @pl.when(even)
    def _():
        for i in range(1, n_shot):
            shot_arrival(lax.rem(s + i, n_shot)).wait_recv()
        traces[row] = jnp.sum(shots[...], axis=0)
        for target in row_targets:
            row_copy(*target).start()

    for side in (0, 1):
        add_halo(0, side, 0)
        send_halo(1, side, 0)

    own_part(1, pl.ds(half, half))
    for side in (0, 1):
        add_halo(1, side, 1)
        send_halo(2, side, 1)

    for i in range(n_rows):
        @pl.when(jnp.logical_not(even & (row == i)))
        def _():
            row_arrival(i).wait_recv()

    for t in (3, 2, 1, 0):
        values = jnp.concatenate([traces[i // 4, pl.ds(4 * (i % 4) + t, 1), :] for i in range(n_grid)], axis=1)
        total = jnp.zeros((rows, oxz.shape[0]), F32)
        for piece in split(values):
            scaled = oy[...] * jnp.broadcast_to(piece, oy.shape)
            total = total + lax.dot_general(scaled, oxz[...], (((1,), (1,)), ((), ())), preferred_element_type=F32)
        inj[t] = total

    inject(0, edges + inner)
    own_part(1, pl.ds(0, half))
    inject(1, edges)
    for side in (0, 1):
        add_halo(1, side, 0)
        send_halo(2, side, 0)
    inject(1, inner)

    for n in (2, 3):
        wait_sent(n - 1)
        own_part(n)
        inject(n, edges + inner)
        for h in (1, 0):
            for side in (0, 1):
                add_halo(n, side, h)
                if n < 3:
                    send_halo(n + 1, side, h)

    wait_sent(0)
    wait_sent(3)

    @pl.when(place == 0)
    def _():
        pair_copy(near[1]).wait_send()

    @pl.when(place == 3)
    def _():
        pair_copy(near[0]).wait_send()

    @pl.when(place == 1)
    def _():
        block_copy(0, 0, near[1]).wait_send()
        block_copy(0, 1, near[0]).wait_send()
        block_copy(1, 2, near[0]).wait_send()

    @pl.when(place == 2)
    def _():
        block_copy(1, 0, near[0]).wait_send()

    @pl.when(even)
    def _():
        for i in range(1, n_shot):
            shot_copy(lax.rem(s + i, n_shot)).wait_send()
        for target in row_targets:
            row_copy(*target).wait_send()


def local(n_grid, n_shot, residuals, encoding, receiver_cells, velocity_term, field_before, field_start):
    shot_rows, samples, local_receivers = residuals.shape
    width, rows, depth = velocity_term.shape
    flat = residuals.reshape(shot_rows * samples, local_receivers)
    n_rec = receiver_cells.shape[1]
    dma = pltpu.SemaphoreType.DMA
    padded = (width + 8, rows, depth)
    vmem = pl.BlockSpec(memory_space=pltpu.VMEM)
    hbm = [
        pltpu.with_memory_space_constraint(a, pltpu.HBM)
        for a in (flat, encoding, receiver_cells, velocity_term, field_before, field_start)
    ]
    fields = pl.pallas_call(
        functools.partial(kernel, n_grid, n_shot),
        out_shape=(pltpu.VMEM(padded, F32), pltpu.VMEM(padded, F32)),
        in_specs=[pl.BlockSpec(memory_space=pltpu.HBM)] * 6,
        out_specs=(vmem, vmem),
        scratch_shapes=[
            pltpu.VMEM((width, rows, depth), F32),
            pltpu.VMEM((4, 2, 4, rows, depth), F32),
            pltpu.VMEM((2, 4, rows, depth // 2), F32),
            pltpu.VMEM((depth, depth), BF16),
            pltpu.VMEM((rows, 2 * rows), BF16),
            pltpu.VMEM(flat.shape, BF16),
            pltpu.VMEM(encoding.shape, BF16),
            pltpu.VMEM(receiver_cells.shape, jnp.int32),
            pltpu.VMEM((n_shot, 8, local_receivers), F32),
            pltpu.VMEM((n_shot, 8, local_receivers), F32),
            pltpu.VMEM((n_shot, 16, local_receivers), F32),
            pltpu.VMEM((n_shot, 16, local_receivers), F32),
            pltpu.VMEM((n_grid // 4, 16, local_receivers), F32),
            pltpu.VMEM((rows, n_rec), BF16),
            pltpu.VMEM((8 * (width + 16), n_rec), BF16),
            pltpu.VMEM((4, rows, 8 * (width + 16)), F32),
            dma((6,)),
            dma((4, 2, 2)),
            dma((4, 2, 2)),
            dma((2,)),
            dma((3,)),
            dma((2,)),
            dma((n_shot,)),
            dma((n_shot,)),
            dma((n_grid // 4, 2)),
            dma((n_grid // 4,)),
            pltpu.SemaphoreType.REGULAR((2,)),
        ],
        compiler_params=pltpu.CompilerParams(
            collective_id=0, has_side_effects=True, vmem_limit_bytes=40 * 1024 * 1024
        ),
        name="window",
    )(*hbm)

    def flush(fa, fb, last, end, sem):
        copies = []
        for i, (field, out) in enumerate(((fa, last), (fb, end))):
            for j in range(4):
                size = width // 4
                copies.append(pltpu.make_async_copy(
                    field.at[pl.ds(4 + j * size, size)], out.at[0, pl.ds(j * size, size)], sem.at[i, j]
                ))
        for copy in copies:
            copy.start()
        for copy in copies:
            copy.wait()

    field = jax.ShapeDtypeStruct(field_start.shape, F32)
    return pl.pallas_call(
        flush,
        out_shape=(field, field),
        in_specs=[vmem, vmem],
        out_specs=[pl.BlockSpec(memory_space=pltpu.HBM)] * 2,
        scratch_shapes=[dma((2, 4))],
        compiler_params=pltpu.CompilerParams(vmem_limit_bytes=16 * 1024 * 1024),
        name="flush",
    )(*fields)


def solution(mesh):
    return jax.shard_map(
        functools.partial(local, mesh.shape["grid"], mesh.shape["shot"]),
        mesh=mesh,
        in_specs=(
            P("shot", None, "grid"),
            P(None, "shot"),
            P(),
            P("grid", None, None),
            P("shot", "grid", None, None),
            P("shot", "grid", None, None),
        ),
        out_specs=(P("shot", "grid", None, None), P("shot", "grid", None, None)),
        check_vma=False,
    )
```

```python
import functools

import jax
import jax.numpy as jnp
from jax import lax
from jax.experimental import pallas as pl
from jax.experimental.pallas import tpu as pltpu
from jax.sharding import PartitionSpec as P

C0, C1, C2, C3, C4 = (-205.0 / 72.0, 8.0 / 5.0, -1.0 / 5.0, 8.0 / 315.0, -1.0 / 560.0)
SCALE = 5040.0
BAND = (8064.0, -1008.0, 128.0, -9.0)
MESH = pl.DeviceIdType.MESH
F32 = jnp.float32
BF16 = jnp.bfloat16


def band_of(distance):
    value = jnp.zeros(distance.shape, F32)
    for j, weight in enumerate(BAND, 1):
        value = jnp.where(distance == j, weight, value)
    return value.astype(BF16)


def iota(shape, dim):
    return lax.broadcasted_iota(jnp.int32, shape, dim)


def split(value):
    high = value.astype(BF16)
    return high, (value - high.astype(F32)).astype(BF16)


def dot(a, b):
    return jnp.dot(a, b, preferred_element_type=F32)


def kernel(
    n_grid, n_shot, res_hbm, enc_hbm, cells_hbm, vt_hbm, before_hbm, start_hbm, fa, fb,
    vt, halo, stage, zmat, ymat, res, enc, cells, part, other, full, shots, traces, oy, oxz, inj,
    relay, load_sem, send_sem, recv_sem, relay_recv, relay_send, pair_sem, block_send, block_recv, shot_send, shot_recv, row_send, row_recv, ready, known,
):
    g = lax.axis_index("grid")
    s = lax.axis_index("shot")
    width, rows, depth = vt.shape
    half = depth // 2
    even = lax.rem(g, 2) == 0
    odd = lax.rem(g, 2) == 1
    has = (g > 0, g < n_grid - 1)
    near = (jnp.maximum(g - 1, 0), jnp.minimum(g + 1, n_grid - 1))
    place = lax.rem(g, 4)
    row = g // 4
    n_rows = n_grid // 4
    flipped = g + jnp.where(place < 2, 2, -2)

    def mate(k):
        return {"grid": jnp.where(lax.rem(k, 2) == lax.rem(s, 2), g, flipped), "shot": k}

    loads = [
        pltpu.make_async_copy(src, dst, load_sem.at[i])
        for i, (src, dst) in enumerate((
            (res_hbm, res),
            (enc_hbm, enc),
            (start_hbm.at[0], fb.at[pl.ds(4, width)]),
            (before_hbm.at[0], fa.at[pl.ds(4, width)]),
            (vt_hbm, vt),
            (cells_hbm, cells),
        ))
    ]
    for load in loads:
        load.start()

    barrier = pltpu.get_barrier_semaphore()

    def greet(**device):
        pl.semaphore_signal(barrier, inc=1, device_id=device, device_id_type=MESH)

    @pl.when(even)
    def _():
        greet(grid=near[1])

        @pl.when(has[0])
        def _():
            greet(grid=near[0])

        for i in range(1, n_shot):
            greet(**mate(lax.rem(s + i, n_shot)))
        for i in range(1, n_rows):
            greet(grid=lax.rem(g + 4 * i, n_grid))

    @pl.when(odd)
    def _():
        for i in range(n_rows):
            greet(grid=lax.rem(g - 1 + 4 * i, n_grid))

    zmat[...] = band_of(jnp.abs(iota((depth, depth), 0) - iota((depth, depth), 1)))
    ymat[...] = band_of(jnp.abs(iota((rows, 2 * rows), 0) - lax.rem(iota((rows, 2 * rows), 1), rows)))
    for f in (fa, fb):
        for p in (0, width + 4):
            f[pl.ds(p, 4)] = jnp.zeros((4, rows, depth), F32)

    def halo_copy(n, side, h, src):
        lanes = pl.ds(h * half, half)
        return pltpu.make_async_remote_copy(
            src_ref=stage.at[side] if (n, h) == (1, 0) else src.at[:, :, lanes],
            dst_ref=halo.at[n, 1 - side, :, :, lanes],
            send_sem=send_sem.at[n, side, h],
            recv_sem=recv_sem.at[n, 1 - side, h],
            device_id={"grid": near[side]},
            device_id_type=MESH,
        )

    def edge_of(n, side):
        if n == 0:
            return start_hbm.at[0, pl.ds(0 if side == 0 else width - 4, 4)]
        f = fb if n % 2 == 0 else fa
        return f.at[pl.ds(4 if side == 0 else width, 4)]

    strip = rows // n_rows
    by_relay = (row, n_rows - 1 - row)
    diagonal = (place == 0, place == 3)
    relay_at = (jnp.minimum(g + 2, n_grid - 1), jnp.maximum(g - 2, 0))

    def source_of(n, side, h, p):
        at = pl.ds(p * strip, strip)
        if (n, h) == (1, 0):
            return stage.at[side, :, at]
        return edge_of(n, side).at[:, at, pl.ds(h * half, half)]

    def direct_piece(n, side, h, p):
        return pltpu.make_async_remote_copy(
            src_ref=source_of(n, side, h, p),
            dst_ref=halo.at[n, 1 - side, :, pl.ds(p * strip, strip), pl.ds(h * half, half)],
            send_sem=send_sem.at[n, side, h],
            recv_sem=recv_sem.at[n, 1 - side, h],
            device_id={"grid": near[side]},
            device_id_type=MESH,
        )

    def relay_piece(n, side, h, p):
        return pltpu.make_async_remote_copy(
            src_ref=source_of(n, side, h, p),
            dst_ref=relay.at[n, h, p],
            send_sem=send_sem.at[n, side, h],
            recv_sem=relay_recv.at[n, h, p],
            device_id={"grid": relay_at[side]},
            device_id_type=MESH,
        )

    def onward_piece(n, side, h, p):
        target = jnp.maximum(g - 3, 0) if side == 0 else jnp.minimum(g + 3, n_grid - 1)
        return pltpu.make_async_remote_copy(
            src_ref=relay.at[n, h, p],
            dst_ref=halo.at[n, 1 - side, :, pl.ds(p * strip, strip), pl.ds(h * half, half)],
            send_sem=relay_send.at[n, h, p],
            recv_sem=recv_sem.at[n, 1 - side, h],
            device_id={"grid": target},
            device_id_type=MESH,
        )

    def each_onward(n, h, act):
        for side in (0, 1):
            @pl.when(place == 2 - side)
            def _():
                for p in range(n_rows - 1):
                    @pl.when(p < by_relay[side])
                    def _():
                        act(n, side, h, p)

    def forward(n, h):
        def act(n, side, h, p):
            relay_piece(n, side, h, p).wait_recv()
            onward_piece(n, side, h, p).start()

        each_onward(n, h, act)

    def send_direct(n, side, h):
        for p in range(n_rows):
            @pl.when(p >= by_relay[side])
            def _():
                direct_piece(n, side, h, p).start()

    def send_by_relay(n, side, h):
        for p in range(n_rows - 1):
            @pl.when(p < by_relay[side])
            def _():
                relay_piece(n, side, h, p).start()

    def send_halo(n, side, h):
        @pl.when(has[side] & jnp.logical_not(diagonal[side]))
        def _():
            halo_copy(n, side, h, edge_of(n, side)).start()

        @pl.when(has[side] & diagonal[side])
        def _():
            send_by_relay(n, side, h)
            send_direct(n, side, h)

    def wait_sent(n):
        for side in (0, 1):
            @pl.when(has[side])
            def _():
                for h in (1, 0):
                    halo_copy(n, side, h, edge_of(n, side)).wait_send()

    def pair_copy(target):
        return pltpu.make_async_remote_copy(
            src_ref=part, dst_ref=other, send_sem=pair_sem.at[0], recv_sem=pair_sem.at[1],
            device_id={"grid": target}, device_id_type=MESH,
        )

    def block_copy(y, sem, target):
        rows_of = full.at[:, pl.ds(8 * y, 8)]
        return pltpu.make_async_remote_copy(
            src_ref=rows_of, dst_ref=rows_of, send_sem=block_send.at[sem], recv_sem=block_recv.at[y],
            device_id={"grid": target}, device_id_type=MESH,
        )

    loads[0].wait()
    loads[1].wait()
    shot_rows, samples = res.shape[0] // 4, 4
    core = lax.rem(g, 2)
    r = iota((8 * n_shot, n_shot), 0)
    pick = jnp.where(r // 8 == iota((8 * n_shot, n_shot), 1), 1.0, 0.0).astype(BF16)
    spread = jnp.where(
        iota((shot_rows, 4 * shot_rows), 0) == iota((shot_rows, 4 * shot_rows), 1) // 4, 1.0, 0.0
    ).astype(BF16)
    weights = dot(dot(pick, enc[...]).astype(BF16), spread)
    wide = (8 * n_shot, 4 * shot_rows)
    weights = jnp.where(lax.rem(iota(wide, 0), 8) - 4 * core == lax.rem(iota(wide, 1), 4), weights, 0.0)
    part[...] = dot(weights.astype(BF16), res[...]).reshape(n_shot, 8, 128)

    @pl.when(odd)
    def _():
        pl.semaphore_wait(barrier, jnp.where(has[1], 2, 1))
        for side in (0, 1):
            @pl.when(has[side])
            def _():
                pl.semaphore_signal(ready.at[1 - side], inc=1, device_id={"grid": near[side]}, device_id_type=MESH)

    for side in (1, 0):
        @pl.when(even & has[side])
        def _():
            pl.semaphore_wait(ready.at[side], 1)
    @pl.when(place == 0)
    def _():
        pair_copy(near[1]).start()

    @pl.when(place == 3)
    def _():
        pair_copy(near[0]).start()

    @pl.when(place == 2)
    def _():
        pl.semaphore_signal(known, inc=1, device_id={"grid": near[1]}, device_id_type=MESH)

    over_y = (place == 2, place == 1)
    for h in (1, 0):
        for side in (0, 1):
            @pl.when(jnp.logical_not(over_y[side] | ((place == 3) & (side == 1))))
            def _():
                send_halo(0, side, h)

    @pl.when(place == 3)
    def _():
        @pl.when(has[1])
        def _():
            send_direct(0, 1, 1)

        pl.semaphore_wait(known, 1)

        @pl.when(has[1])
        def _():
            send_by_relay(0, 1, 1)
            send_direct(0, 1, 0)
            send_by_relay(0, 1, 0)

    @pl.when(place == 1)
    def _():
        pair_copy(near[0]).wait_recv()
        full[:, pl.ds(0, 8)] = part[...] + other[...]
        block_copy(0, 0, near[1]).start()
        block_copy(0, 1, near[0]).start()

    @pl.when(place == 2)
    def _():
        pair_copy(near[1]).wait_recv()
        full[:, pl.ds(8, 8)] = part[...] + other[...]
        block_copy(1, 0, near[0]).start()

    for h in (1, 0):
        for side in (0, 1):
            @pl.when(over_y[side])
            def _():
                send_halo(0, side, h)

    for load in loads[2:]:
        load.wait()

    n_rec = cells.shape[1]
    oy[...] = jnp.where(iota((rows, n_rec), 0) == cells[1:2, :], 1.0, 0.0).astype(BF16)
    spot = (cells[0:1, :] - g * width + 8) * 8 + cells[2:3, :]
    oxz[...] = jnp.where(iota(oxz.shape, 0) == spot, 1.0, 0.0).astype(BF16)

    def own_part(n, lanes=pl.ds(0, depth)):
        cur, nxt = (fb, fa) if n % 2 == 0 else (fa, fb)

        def plane(x, carry):
            high, low = split(cur[x + 4])
            along = zmat[:, lanes]
            across = dot(jnp.concatenate([high, low], axis=1), jnp.concatenate([along, along], axis=0))
            at = slice(lanes.start, lanes.start + lanes.size)
            across = across + dot(ymat[...], jnp.concatenate([high[:, at], low[:, at]], axis=0))
            u = cur[x + 4, :, lanes]
            total = (3.0 * C0) * u + across * (1.0 / SCALE)
            for j, weight in enumerate((C1, C2, C3, C4), 1):
                total = total + weight * (cur[x + 4 + j, :, lanes] + cur[x + 4 - j, :, lanes])
            nxt[x + 4, :, lanes] = 2.0 * u - nxt[x + 4, :, lanes] + vt[x, :, lanes] * total
            return carry

        lax.fori_loop(0, width, plane, 0)

    def add_halo(n, side, h):
        nxt = fa if n % 2 == 0 else fb
        lanes = pl.ds(h * half, half)

        @pl.when(has[side])
        def _():
            halo_copy(n, 1 - side, h, edge_of(n, 1 - side)).wait_recv()
            if (n, h) == (1, 0):
                for p in range(4):
                    x = p - 4 if side == 0 else width + p
                    halo[n, side, p, :, lanes] = halo[n, side, p, :, lanes] + traces_at(0, x)
            layer = [halo[n, side, 4 - d if side == 0 else d - 1, :, lanes] for d in (1, 2, 3, 4)]
            for i in range(4):
                x = i if side == 0 else width - 1 - i
                total = C4 * layer[3 - i]
                for j, weight in ((1, C1), (2, C2), (3, C3)):
                    if j > i:
                        total = total + weight * layer[j - i - 1]
                value = nxt[x + 4, :, lanes] + vt[x, :, lanes] * total
                nxt[x + 4, :, lanes] = value
                if (n, h) == (0, 0):
                    stage[side, i if side == 0 else 3 - i] = value

    def traces_at(n, x):
        tile, lane = divmod(8 * (x + 8), half)
        values = inj[3 - n, :, pl.ds(tile * half, half)]
        moved = values if lane == 0 else pltpu.roll(values, half - lane, 1)
        return jnp.where(iota((rows, half), 1) < 8, moved, 0.0)

    def inject(n, planes):
        nxt = fa if n % 2 == 0 else fb
        for x in planes:
            nxt[x + 4, :, pl.ds(0, half)] = nxt[x + 4, :, pl.ds(0, half)] + traces_at(n, x)

    edges = list(range(4)) + list(range(width - 4, width))
    inner = list(range(4, width - 4))

    own_part(0)

    def shot_copy(k):
        return pltpu.make_async_remote_copy(
            src_ref=full.at[k], dst_ref=shots.at[s], send_sem=shot_send.at[k], recv_sem=shot_recv.at[s],
            device_id=mate(k), device_id_type=MESH,
        )

    def shot_arrival(k):
        return pltpu.make_async_remote_copy(
            src_ref=full.at[k], dst_ref=shots.at[k], send_sem=shot_send.at[k], recv_sem=shot_recv.at[k],
            device_id=mate(k), device_id_type=MESH,
        )

    def row_copy(i, core):
        return pltpu.make_async_remote_copy(
            src_ref=traces.at[row], dst_ref=traces.at[row], send_sem=row_send.at[i, core], recv_sem=row_recv.at[row],
            device_id={"grid": lax.rem(g + 4 * i + core, n_grid)}, device_id_type=MESH,
        )

    def row_arrival(i):
        return pltpu.make_async_remote_copy(
            src_ref=traces.at[i], dst_ref=traces.at[i], send_sem=row_send.at[0, 0], recv_sem=row_recv.at[i],
            device_id={"grid": near[0]}, device_id_type=MESH,
        )

    row_targets = [(i, core) for i in range(n_rows) for core in (0, 1) if i or core]

    @pl.when(place == 1)
    def _():
        block_copy(1, 2, near[1]).wait_recv()
        block_copy(1, 2, near[0]).start()

    @pl.when(place == 0)
    def _():
        block_copy(0, 0, near[1]).wait_recv()
        block_copy(1, 0, near[1]).wait_recv()

    @pl.when(place == 2)
    def _():
        block_copy(0, 0, near[0]).wait_recv()

    @pl.when(even)
    def _():
        shots[s] = full[s]
        pl.semaphore_wait(barrier, n_shot - 1 + 2 * n_rows - 1)
        for i in range(1, n_shot):
            shot_copy(lax.rem(s + i, n_shot)).start()

    forward(0, 1)
    for side in (0, 1):
        add_halo(0, side, 1)
        send_halo(1, side, 1)
    forward(0, 0)

    @pl.when(even)
    def _():
        for i in range(1, n_shot):
            shot_arrival(lax.rem(s + i, n_shot)).wait_recv()
        traces[row] = jnp.sum(shots[...], axis=0)
        for target in row_targets:
            row_copy(*target).start()

    for side in (0, 1):
        add_halo(0, side, 0)
        send_halo(1, side, 0)

    own_part(1, pl.ds(half, half))
    forward(1, 1)
    for side in (0, 1):
        add_halo(1, side, 1)
        send_halo(2, side, 1)
    forward(1, 0)

    for i in range(n_rows):
        @pl.when(jnp.logical_not(even & (row == i)))
        def _():
            row_arrival(i).wait_recv()

    for t in (3, 2, 1, 0):
        values = jnp.concatenate([traces[i // 4, pl.ds(4 * (i % 4) + t, 1), :] for i in range(n_grid)], axis=1)
        total = jnp.zeros((rows, oxz.shape[0]), F32)
        for piece in split(values):
            scaled = oy[...] * jnp.broadcast_to(piece, oy.shape)
            total = total + lax.dot_general(scaled, oxz[...], (((1,), (1,)), ((), ())), preferred_element_type=F32)
        inj[t] = total

    inject(0, edges + inner)
    own_part(1, pl.ds(0, half))
    inject(1, edges)
    for side in (0, 1):
        add_halo(1, side, 0)
        send_halo(2, side, 0)
    inject(1, inner)

    for n in (2, 3):
        wait_sent(n - 1)
        own_part(n)
        inject(n, edges + inner)
        for h in (1, 0):
            forward(n, h)
            for side in (0, 1):
                add_halo(n, side, h)
                if n < 3:
                    send_halo(n + 1, side, h)

    wait_sent(0)
    for n in range(4):
        for h in (1, 0):
            each_onward(n, h, lambda *which: onward_piece(*which).wait_send())
    wait_sent(3)

    @pl.when(place == 0)
    def _():
        pair_copy(near[1]).wait_send()

    @pl.when(place == 3)
    def _():
        pair_copy(near[0]).wait_send()

    @pl.when(place == 1)
    def _():
        block_copy(0, 0, near[1]).wait_send()
        block_copy(0, 1, near[0]).wait_send()
        block_copy(1, 2, near[0]).wait_send()

    @pl.when(place == 2)
    def _():
        block_copy(1, 0, near[0]).wait_send()

    @pl.when(even)
    def _():
        for i in range(1, n_shot):
            shot_copy(lax.rem(s + i, n_shot)).wait_send()
        for target in row_targets:
            row_copy(*target).wait_send()


def local(n_grid, n_shot, residuals, encoding, receiver_cells, velocity_term, field_before, field_start):
    shot_rows, samples, local_receivers = residuals.shape
    width, rows, depth = velocity_term.shape
    flat = residuals.reshape(shot_rows * samples, local_receivers)
    n_rec = receiver_cells.shape[1]
    dma = pltpu.SemaphoreType.DMA
    padded = (width + 8, rows, depth)
    vmem = pl.BlockSpec(memory_space=pltpu.VMEM)
    hbm = [
        pltpu.with_memory_space_constraint(a, pltpu.HBM)
        for a in (flat, encoding, receiver_cells, velocity_term, field_before, field_start)
    ]
    fields = pl.pallas_call(
        functools.partial(kernel, n_grid, n_shot),
        out_shape=(pltpu.VMEM(padded, F32), pltpu.VMEM(padded, F32)),
        in_specs=[pl.BlockSpec(memory_space=pltpu.HBM)] * 6,
        out_specs=(vmem, vmem),
        scratch_shapes=[
            pltpu.VMEM((width, rows, depth), F32),
            pltpu.VMEM((4, 2, 4, rows, depth), F32),
            pltpu.VMEM((2, 4, rows, depth // 2), F32),
            pltpu.VMEM((depth, depth), BF16),
            pltpu.VMEM((rows, 2 * rows), BF16),
            pltpu.VMEM(flat.shape, BF16),
            pltpu.VMEM(encoding.shape, BF16),
            pltpu.VMEM(receiver_cells.shape, jnp.int32),
            pltpu.VMEM((n_shot, 8, local_receivers), F32),
            pltpu.VMEM((n_shot, 8, local_receivers), F32),
            pltpu.VMEM((n_shot, 16, local_receivers), F32),
            pltpu.VMEM((n_shot, 16, local_receivers), F32),
            pltpu.VMEM((n_grid // 4, 16, local_receivers), F32),
            pltpu.VMEM((rows, n_rec), BF16),
            pltpu.VMEM((8 * (width + 16), n_rec), BF16),
            pltpu.VMEM((4, rows, 8 * (width + 16)), F32),
            pltpu.VMEM((4, 2, n_grid // 4 - 1, 4, rows // (n_grid // 4), depth // 2), F32),
            dma((6,)),
            dma((4, 2, 2)),
            dma((4, 2, 2)),
            dma((4, 2, n_grid // 4 - 1)),
            dma((4, 2, n_grid // 4 - 1)),
            dma((2,)),
            dma((3,)),
            dma((2,)),
            dma((n_shot,)),
            dma((n_shot,)),
            dma((n_grid // 4, 2)),
            dma((n_grid // 4,)),
            pltpu.SemaphoreType.REGULAR((2,)),
            pltpu.SemaphoreType.REGULAR,
        ],
        compiler_params=pltpu.CompilerParams(
            collective_id=0, has_side_effects=True, vmem_limit_bytes=40 * 1024 * 1024
        ),
        name="window",
    )(*hbm)

    def flush(fa, fb, last, end, sem):
        copies = []
        for i, (field, out) in enumerate(((fa, last), (fb, end))):
            for j in range(4):
                size = width // 4
                copies.append(pltpu.make_async_copy(
                    field.at[pl.ds(4 + j * size, size)], out.at[0, pl.ds(j * size, size)], sem.at[i, j]
                ))
        for copy in copies:
            copy.start()
        for copy in copies:
            copy.wait()

    field = jax.ShapeDtypeStruct(field_start.shape, F32)
    return pl.pallas_call(
        flush,
        out_shape=(field, field),
        in_specs=[vmem, vmem],
        out_specs=[pl.BlockSpec(memory_space=pltpu.HBM)] * 2,
        scratch_shapes=[dma((2, 4))],
        compiler_params=pltpu.CompilerParams(vmem_limit_bytes=16 * 1024 * 1024),
        name="flush",
    )(*fields)


def solution(mesh):
    return jax.shard_map(
        functools.partial(local, mesh.shape["grid"], mesh.shape["shot"]),
        mesh=mesh,
        in_specs=(
            P("shot", None, "grid"),
            P(None, "shot"),
            P(),
            P("grid", None, None),
            P("shot", "grid", None, None),
            P("shot", "grid", None, None),
        ),
        out_specs=(P("shot", "grid", None, None), P("shot", "grid", None, None)),
        check_vma=False,
    )
```

```python
import functools

import jax
import jax.numpy as jnp
from jax import lax
from jax.experimental import pallas as pl
from jax.experimental.pallas import tpu as pltpu
from jax.sharding import PartitionSpec as P

C0, C1, C2, C3, C4 = (-205.0 / 72.0, 8.0 / 5.0, -1.0 / 5.0, 8.0 / 315.0, -1.0 / 560.0)
SCALE = 5040.0
BAND = (8064.0, -1008.0, 128.0, -9.0)
MESH = pl.DeviceIdType.MESH
F32 = jnp.float32
BF16 = jnp.bfloat16


def band_of(distance):
    value = jnp.zeros(distance.shape, F32)
    for j, weight in enumerate(BAND, 1):
        value = jnp.where(distance == j, weight, value)
    return value.astype(BF16)


def iota(shape, dim):
    return lax.broadcasted_iota(jnp.int32, shape, dim)


def split(value):
    high = value.astype(BF16)
    return high, (value - high.astype(F32)).astype(BF16)


def dot(a, b):
    return jnp.dot(a, b, preferred_element_type=F32)


def kernel(
    n_grid, n_shot, res_hbm, enc_hbm, cells_hbm, vt_hbm, before_hbm, start_hbm, fa, fb,
    vt, halo, stage, zmat, ymat, res, enc, cells, part, other, full, shots, traces, oy, oxz, inj,
    relay, load_sem, send_sem, recv_sem, relay_recv, relay_send, pair_sem, block_send, block_recv, shot_send, shot_recv, row_send, row_recv, ready, known,
):
    g = lax.axis_index("grid")
    s = lax.axis_index("shot")
    width, rows, depth = vt.shape
    half = depth // 2
    even = lax.rem(g, 2) == 0
    odd = lax.rem(g, 2) == 1
    has = (g > 0, g < n_grid - 1)
    near = (jnp.maximum(g - 1, 0), jnp.minimum(g + 1, n_grid - 1))
    place = lax.rem(g, 4)
    row = g // 4
    n_rows = n_grid // 4
    flipped = g + jnp.where(place < 2, 2, -2)

    def mate(k):
        return {"grid": jnp.where(lax.rem(k, 2) == lax.rem(s, 2), g, flipped), "shot": k}

    loads = [
        pltpu.make_async_copy(src, dst, load_sem.at[i])
        for i, (src, dst) in enumerate((
            (res_hbm, res),
            (enc_hbm, enc),
            (start_hbm.at[0], fb.at[pl.ds(4, width)]),
            (before_hbm.at[0], fa.at[pl.ds(4, width)]),
            (vt_hbm, vt),
            (cells_hbm, cells),
        ))
    ]
    for load in loads:
        load.start()

    barrier = pltpu.get_barrier_semaphore()

    def greet(**device):
        pl.semaphore_signal(barrier, inc=1, device_id=device, device_id_type=MESH)

    @pl.when(even)
    def _():
        greet(grid=near[1])

        @pl.when(has[0])
        def _():
            greet(grid=near[0])

        for i in range(1, n_shot):
            greet(**mate(lax.rem(s + i, n_shot)))
        for i in range(1, n_rows):
            greet(grid=lax.rem(g + 4 * i, n_grid))

    @pl.when(odd)
    def _():
        for i in range(n_rows):
            greet(grid=lax.rem(g - 1 + 4 * i, n_grid))

    zmat[...] = band_of(jnp.abs(iota((depth, depth), 0) - iota((depth, depth), 1)))
    ymat[...] = band_of(jnp.abs(iota((rows, 2 * rows), 0) - lax.rem(iota((rows, 2 * rows), 1), rows)))
    for f in (fa, fb):
        for p in (0, width + 4):
            f[pl.ds(p, 4)] = jnp.zeros((4, rows, depth), F32)

    def halo_copy(n, side, h, src):
        lanes = pl.ds(h * half, half)
        return pltpu.make_async_remote_copy(
            src_ref=stage.at[side] if (n, h) == (1, 0) else src.at[:, :, lanes],
            dst_ref=halo.at[n, 1 - side, :, :, lanes],
            send_sem=send_sem.at[n, side, h],
            recv_sem=recv_sem.at[n, 1 - side, h],
            device_id={"grid": near[side]},
            device_id_type=MESH,
        )

    def edge_of(n, side):
        if n == 0:
            return start_hbm.at[0, pl.ds(0 if side == 0 else width - 4, 4)]
        f = fb if n % 2 == 0 else fa
        return f.at[pl.ds(4 if side == 0 else width, 4)]

    strip = rows // n_rows
    by_relay = (row, n_rows - 1 - row)
    diagonal = (place == 0, place == 3)
    relay_at = (jnp.minimum(g + 2, n_grid - 1), jnp.maximum(g - 2, 0))

    def source_of(n, side, h, p):
        at = pl.ds(p * strip, strip)
        if (n, h) == (1, 0):
            return stage.at[side, :, at]
        return edge_of(n, side).at[:, at, pl.ds(h * half, half)]

    def direct_piece(n, side, h, p):
        return pltpu.make_async_remote_copy(
            src_ref=source_of(n, side, h, p),
            dst_ref=halo.at[n, 1 - side, :, pl.ds(p * strip, strip), pl.ds(h * half, half)],
            send_sem=send_sem.at[n, side, h],
            recv_sem=recv_sem.at[n, 1 - side, h],
            device_id={"grid": near[side]},
            device_id_type=MESH,
        )

    def relay_piece(n, side, h, p):
        return pltpu.make_async_remote_copy(
            src_ref=source_of(n, side, h, p),
            dst_ref=relay.at[n, h, p],
            send_sem=send_sem.at[n, side, h],
            recv_sem=relay_recv.at[n, h, p],
            device_id={"grid": relay_at[side]},
            device_id_type=MESH,
        )

    def onward_piece(n, side, h, p):
        target = jnp.maximum(g - 3, 0) if side == 0 else jnp.minimum(g + 3, n_grid - 1)
        return pltpu.make_async_remote_copy(
            src_ref=relay.at[n, h, p],
            dst_ref=halo.at[n, 1 - side, :, pl.ds(p * strip, strip), pl.ds(h * half, half)],
            send_sem=relay_send.at[n, h, p],
            recv_sem=recv_sem.at[n, 1 - side, h],
            device_id={"grid": target},
            device_id_type=MESH,
        )

    def each_onward(n, h, act):
        for side in (0, 1):
            @pl.when(place == 2 - side)
            def _():
                for p in range(n_rows - 1):
                    @pl.when(p < by_relay[side])
                    def _():
                        act(n, side, h, p)

    def forward(n, h):
        def act(n, side, h, p):
            relay_piece(n, side, h, p).wait_recv()
            onward_piece(n, side, h, p).start()

        each_onward(n, h, act)

    def send_direct(n, side, h):
        for p in range(n_rows):
            @pl.when(p >= by_relay[side])
            def _():
                direct_piece(n, side, h, p).start()

    def send_by_relay(n, side, h):
        for p in range(n_rows - 1):
            @pl.when(p < by_relay[side])
            def _():
                relay_piece(n, side, h, p).start()

    def send_halo(n, side, h):
        @pl.when(has[side] & jnp.logical_not(diagonal[side]))
        def _():
            halo_copy(n, side, h, edge_of(n, side)).start()

        @pl.when(has[side] & diagonal[side])
        def _():
            send_by_relay(n, side, h)
            send_direct(n, side, h)

    def wait_half_sent(n, side, h):
        @pl.when(has[side])
        def _():
            halo_copy(n, side, h, edge_of(n, side)).wait_send()

    def wait_sent(n):
        for side in (0, 1):
            for h in (1, 0):
                wait_half_sent(n, side, h)

    def pair_copy(target):
        return pltpu.make_async_remote_copy(
            src_ref=part, dst_ref=other, send_sem=pair_sem.at[0], recv_sem=pair_sem.at[1],
            device_id={"grid": target}, device_id_type=MESH,
        )

    def block_copy(y, sem, target):
        rows_of = full.at[:, pl.ds(8 * y, 8)]
        return pltpu.make_async_remote_copy(
            src_ref=rows_of, dst_ref=rows_of, send_sem=block_send.at[sem], recv_sem=block_recv.at[y],
            device_id={"grid": target}, device_id_type=MESH,
        )

    loads[0].wait()
    loads[1].wait()
    shot_rows, samples = res.shape[0] // 4, 4
    core = lax.rem(g, 2)
    r = iota((8 * n_shot, n_shot), 0)
    pick = jnp.where(r // 8 == iota((8 * n_shot, n_shot), 1), 1.0, 0.0).astype(BF16)
    spread = jnp.where(
        iota((shot_rows, 4 * shot_rows), 0) == iota((shot_rows, 4 * shot_rows), 1) // 4, 1.0, 0.0
    ).astype(BF16)
    weights = dot(dot(pick, enc[...]).astype(BF16), spread)
    wide = (8 * n_shot, 4 * shot_rows)
    weights = jnp.where(lax.rem(iota(wide, 0), 8) - 4 * core == lax.rem(iota(wide, 1), 4), weights, 0.0)
    part[...] = dot(weights.astype(BF16), res[...]).reshape(n_shot, 8, 128)

    @pl.when(odd)
    def _():
        pl.semaphore_wait(barrier, jnp.where(has[1], 2, 1))
        for side in (0, 1):
            @pl.when(has[side])
            def _():
                pl.semaphore_signal(ready.at[1 - side], inc=1, device_id={"grid": near[side]}, device_id_type=MESH)

    for side in (1, 0):
        @pl.when(even & has[side])
        def _():
            pl.semaphore_wait(ready.at[side], 1)
    @pl.when(place == 0)
    def _():
        pair_copy(near[1]).start()

    @pl.when(place == 3)
    def _():
        pair_copy(near[0]).start()

    @pl.when(place == 2)
    def _():
        pl.semaphore_signal(known, inc=1, device_id={"grid": near[1]}, device_id_type=MESH)

    over_y = (place == 2, place == 1)
    for side in (0, 1):
        @pl.when(jnp.logical_not(over_y[side] | ((place == 3) & (side == 1))))
        def _():
            send_halo(0, side, 1)

    @pl.when(place == 3)
    def _():
        @pl.when(has[1])
        def _():
            send_direct(0, 1, 1)

        pl.semaphore_wait(known, 1)

        @pl.when(has[1])
        def _():
            send_by_relay(0, 1, 1)

    @pl.when(place == 1)
    def _():
        pair_copy(near[0]).wait_recv()
        full[:, pl.ds(0, 8)] = part[...] + other[...]
        block_copy(0, 0, near[1]).start()
        block_copy(0, 1, near[0]).start()

    @pl.when(place == 2)
    def _():
        pair_copy(near[1]).wait_recv()
        full[:, pl.ds(8, 8)] = part[...] + other[...]
        block_copy(1, 0, near[0]).start()

    for side in (0, 1):
        @pl.when(over_y[side])
        def _():
            send_halo(0, side, 1)

    for load in loads[2:]:
        load.wait()

    def own_part(n, lanes=pl.ds(0, depth)):
        cur, nxt = (fb, fa) if n % 2 == 0 else (fa, fb)

        def plane(x, carry):
            high, low = split(cur[x + 4])
            along = zmat[:, lanes]
            across = dot(jnp.concatenate([high, low], axis=1), jnp.concatenate([along, along], axis=0))
            at = slice(lanes.start, lanes.start + lanes.size)
            across = across + dot(ymat[...], jnp.concatenate([high[:, at], low[:, at]], axis=0))
            u = cur[x + 4, :, lanes]
            total = (3.0 * C0) * u + across * (1.0 / SCALE)
            for j, weight in enumerate((C1, C2, C3, C4), 1):
                total = total + weight * (cur[x + 4 + j, :, lanes] + cur[x + 4 - j, :, lanes])
            nxt[x + 4, :, lanes] = 2.0 * u - nxt[x + 4, :, lanes] + vt[x, :, lanes] * total
            return carry

        lax.fori_loop(0, width, plane, 0)

    def add_halo(n, side, h):
        nxt = fa if n % 2 == 0 else fb
        lanes = pl.ds(h * half, half)

        @pl.when(has[side])
        def _():
            halo_copy(n, 1 - side, h, edge_of(n, 1 - side)).wait_recv()
            if (n, h) == (1, 0):
                for p in range(4):
                    x = p - 4 if side == 0 else width + p
                    halo[n, side, p, :, lanes] = halo[n, side, p, :, lanes] + traces_at(0, x)
            layer = [halo[n, side, 4 - d if side == 0 else d - 1, :, lanes] for d in (1, 2, 3, 4)]
            for i in range(4):
                x = i if side == 0 else width - 1 - i
                total = C4 * layer[3 - i]
                for j, weight in ((1, C1), (2, C2), (3, C3)):
                    if j > i:
                        total = total + weight * layer[j - i - 1]
                value = nxt[x + 4, :, lanes] + vt[x, :, lanes] * total
                nxt[x + 4, :, lanes] = value
                if (n, h) == (0, 0):
                    stage[side, i if side == 0 else 3 - i] = value

    def traces_at(n, x):
        tile, lane = divmod(8 * (x + 8), half)
        values = inj[3 - n, :, pl.ds(tile * half, half)]
        moved = values if lane == 0 else pltpu.roll(values, half - lane, 1)
        return jnp.where(iota((rows, half), 1) < 8, moved, 0.0)

    def inject(n, planes):
        nxt = fa if n % 2 == 0 else fb
        for x in planes:
            nxt[x + 4, :, pl.ds(0, half)] = nxt[x + 4, :, pl.ds(0, half)] + traces_at(n, x)

    edges = list(range(4)) + list(range(width - 4, width))
    inner = list(range(4, width - 4))

    own_part(0)
    for side in (0, 1):
        send_halo(0, side, 0)

    def shot_copy(k):
        return pltpu.make_async_remote_copy(
            src_ref=full.at[k], dst_ref=shots.at[s], send_sem=shot_send.at[k], recv_sem=shot_recv.at[s],
            device_id=mate(k), device_id_type=MESH,
        )

    def shot_arrival(k):
        return pltpu.make_async_remote_copy(
            src_ref=full.at[k], dst_ref=shots.at[k], send_sem=shot_send.at[k], recv_sem=shot_recv.at[k],
            device_id=mate(k), device_id_type=MESH,
        )

    def row_copy(i, core):
        return pltpu.make_async_remote_copy(
            src_ref=traces.at[row], dst_ref=traces.at[row], send_sem=row_send.at[i, core], recv_sem=row_recv.at[row],
            device_id={"grid": lax.rem(g + 4 * i + core, n_grid)}, device_id_type=MESH,
        )

    def row_arrival(i):
        return pltpu.make_async_remote_copy(
            src_ref=traces.at[i], dst_ref=traces.at[i], send_sem=row_send.at[0, 0], recv_sem=row_recv.at[i],
            device_id={"grid": near[0]}, device_id_type=MESH,
        )

    row_targets = [(i, core) for i in range(n_rows) for core in (0, 1) if i or core]

    @pl.when(place == 1)
    def _():
        block_copy(1, 2, near[1]).wait_recv()
        block_copy(1, 2, near[0]).start()

    @pl.when(place == 0)
    def _():
        block_copy(0, 0, near[1]).wait_recv()
        block_copy(1, 0, near[1]).wait_recv()

    @pl.when(place == 2)
    def _():
        block_copy(0, 0, near[0]).wait_recv()

    @pl.when(even)
    def _():
        shots[s] = full[s]
        pl.semaphore_wait(barrier, n_shot - 1 + 2 * n_rows - 1)
        for i in range(1, n_shot):
            shot_copy(lax.rem(s + i, n_shot)).start()

    n_rec = cells.shape[1]
    oy[...] = jnp.where(iota((rows, n_rec), 0) == cells[1:2, :], 1.0, 0.0).astype(BF16)
    spot = ((cells[0:1, :] - g * width + 8) * 8 + cells[2:3, :]).astype(F32)
    spot = jnp.transpose(jnp.broadcast_to(spot, (128, n_rec)))
    for tile in range(oxz.shape[1] // 128):
        lane = (iota((n_rec, 128), 1) + 128 * tile).astype(F32)
        oxz[:, pl.ds(128 * tile, 128)] = jnp.where(spot == lane, 1.0, 0.0).astype(BF16)

    forward(0, 1)
    for side in (0, 1):
        add_halo(0, side, 1)
        send_halo(1, side, 1)
    forward(0, 0)

    for side in (0, 1):
        add_halo(0, side, 0)
        send_halo(1, side, 0)

    @pl.when(even)
    def _():
        for i in range(1, n_shot):
            shot_arrival(lax.rem(s + i, n_shot)).wait_recv()
        traces[row] = jnp.sum(shots[...], axis=0)
        for target in row_targets:
            row_copy(*target).start()

    own_part(1, pl.ds(half, half))
    forward(1, 1)
    for side in (0, 1):
        add_halo(1, side, 1)
        send_halo(2, side, 1)
    forward(1, 0)

    for i in range(n_rows):
        @pl.when(jnp.logical_not(even & (row == i)))
        def _():
            row_arrival(i).wait_recv()

    def build(t):
        values = jnp.concatenate([traces[i // 4, pl.ds(4 * (i % 4) + t, 1), :] for i in range(n_grid)], axis=1)
        scaled = [oy[...] * jnp.broadcast_to(piece, oy.shape) for piece in split(values)]
        total = dot(jnp.concatenate(scaled, axis=0), oxz[...])
        inj[t] = total[:rows] + total[rows:]

    build(3)
    build(2)
    inject(0, edges + inner)
    own_part(1, pl.ds(0, half))
    inject(1, edges)
    for side in (0, 1):
        add_halo(1, side, 0)
        send_halo(2, side, 0)
    inject(1, inner)
    build(1)
    build(0)

    for n in (2, 3):
        wait_sent(n - 1)
        own_part(n)
        inject(n, edges + inner)
        for h in (1, 0):
            forward(n, h)
            for side in (0, 1):
                add_halo(n, side, h)
                if n < 3:
                    send_halo(n + 1, side, h)

    wait_sent(0)
    for n in range(4):
        for h in (1, 0):
            each_onward(n, h, lambda *which: onward_piece(*which).wait_send())
    wait_sent(3)

    @pl.when(place == 0)
    def _():
        pair_copy(near[1]).wait_send()

    @pl.when(place == 3)
    def _():
        pair_copy(near[0]).wait_send()

    @pl.when(place == 1)
    def _():
        block_copy(0, 0, near[1]).wait_send()
        block_copy(0, 1, near[0]).wait_send()
        block_copy(1, 2, near[0]).wait_send()

    @pl.when(place == 2)
    def _():
        block_copy(1, 0, near[0]).wait_send()

    @pl.when(even)
    def _():
        for i in range(1, n_shot):
            shot_copy(lax.rem(s + i, n_shot)).wait_send()
        for target in row_targets:
            row_copy(*target).wait_send()


def local(n_grid, n_shot, residuals, encoding, receiver_cells, velocity_term, field_before, field_start):
    shot_rows, samples, local_receivers = residuals.shape
    width, rows, depth = velocity_term.shape
    flat = residuals.reshape(shot_rows * samples, local_receivers)
    n_rec = receiver_cells.shape[1]
    dma = pltpu.SemaphoreType.DMA
    padded = (width + 8, rows, depth)
    vmem = pl.BlockSpec(memory_space=pltpu.VMEM)
    hbm = [
        pltpu.with_memory_space_constraint(a, pltpu.HBM)
        for a in (flat, encoding, receiver_cells, velocity_term, field_before, field_start)
    ]
    fields = pl.pallas_call(
        functools.partial(kernel, n_grid, n_shot),
        out_shape=(pltpu.VMEM(padded, F32), pltpu.VMEM(padded, F32)),
        in_specs=[pl.BlockSpec(memory_space=pltpu.HBM)] * 6,
        out_specs=(vmem, vmem),
        scratch_shapes=[
            pltpu.VMEM((width, rows, depth), F32),
            pltpu.VMEM((4, 2, 4, rows, depth), F32),
            pltpu.VMEM((2, 4, rows, depth // 2), F32),
            pltpu.VMEM((depth, depth), BF16),
            pltpu.VMEM((rows, 2 * rows), BF16),
            pltpu.VMEM(flat.shape, BF16),
            pltpu.VMEM(encoding.shape, BF16),
            pltpu.VMEM(receiver_cells.shape, jnp.int32),
            pltpu.VMEM((n_shot, 8, local_receivers), F32),
            pltpu.VMEM((n_shot, 8, local_receivers), F32),
            pltpu.VMEM((n_shot, 16, local_receivers), F32),
            pltpu.VMEM((n_shot, 16, local_receivers), F32),
            pltpu.VMEM((n_grid // 4, 16, local_receivers), F32),
            pltpu.VMEM((rows, n_rec), BF16),
            pltpu.VMEM((n_rec, 8 * (width + 16)), BF16),
            pltpu.VMEM((4, rows, 8 * (width + 16)), F32),
            pltpu.VMEM((4, 2, n_grid // 4 - 1, 4, rows // (n_grid // 4), depth // 2), F32),
            dma((6,)),
            dma((4, 2, 2)),
            dma((4, 2, 2)),
            dma((4, 2, n_grid // 4 - 1)),
            dma((4, 2, n_grid // 4 - 1)),
            dma((2,)),
            dma((3,)),
            dma((2,)),
            dma((n_shot,)),
            dma((n_shot,)),
            dma((n_grid // 4, 2)),
            dma((n_grid // 4,)),
            pltpu.SemaphoreType.REGULAR((2,)),
            pltpu.SemaphoreType.REGULAR,
        ],
        compiler_params=pltpu.CompilerParams(
            collective_id=0, has_side_effects=True, vmem_limit_bytes=40 * 1024 * 1024
        ),
        name="window",
    )(*hbm)

    def flush(fa, fb, last, end, sem):
        copies = []
        for i, (field, out) in enumerate(((fa, last), (fb, end))):
            for j in range(4):
                size = width // 4
                copies.append(pltpu.make_async_copy(
                    field.at[pl.ds(4 + j * size, size)], out.at[0, pl.ds(j * size, size)], sem.at[i, j]
                ))
        for copy in copies:
            copy.start()
        for copy in copies:
            copy.wait()

    field = jax.ShapeDtypeStruct(field_start.shape, F32)
    return pl.pallas_call(
        flush,
        out_shape=(field, field),
        in_specs=[vmem, vmem],
        out_specs=[pl.BlockSpec(memory_space=pltpu.HBM)] * 2,
        scratch_shapes=[dma((2, 4))],
        compiler_params=pltpu.CompilerParams(vmem_limit_bytes=16 * 1024 * 1024),
        name="flush",
    )(*fields)


def solution(mesh):
    return jax.shard_map(
        functools.partial(local, mesh.shape["grid"], mesh.shape["shot"]),
        mesh=mesh,
        in_specs=(
            P("shot", None, "grid"),
            P(None, "shot"),
            P(),
            P("grid", None, None),
            P("shot", "grid", None, None),
            P("shot", "grid", None, None),
        ),
        out_specs=(P("shot", "grid", None, None), P("shot", "grid", None, None)),
        check_vma=False,
    )
```

```python
import functools

import jax
import jax.numpy as jnp
from jax import lax
from jax.experimental import pallas as pl
from jax.experimental.pallas import tpu as pltpu
from jax.sharding import PartitionSpec as P

C0, C1, C2, C3, C4 = (-205.0 / 72.0, 8.0 / 5.0, -1.0 / 5.0, 8.0 / 315.0, -1.0 / 560.0)
SCALE = 5040.0
BAND = (8064.0, -1008.0, 128.0, -9.0)
MESH = pl.DeviceIdType.MESH
F32 = jnp.float32
BF16 = jnp.bfloat16


def band_of(distance):
    value = jnp.zeros(distance.shape, F32)
    for j, weight in enumerate(BAND, 1):
        value = jnp.where(distance == j, weight, value)
    return value.astype(BF16)


def iota(shape, dim):
    return lax.broadcasted_iota(jnp.int32, shape, dim)


def split(value):
    high = value.astype(BF16)
    return high, (value - high.astype(F32)).astype(BF16)


def dot(a, b):
    return jnp.dot(a, b, preferred_element_type=F32)


def kernel(
    n_grid, n_shot, res_hbm, enc_hbm, cells_hbm, vt_hbm, before_hbm, start_hbm, fa, fb,
    vt, halo, stage, zmat, ymat, res, enc, cells, part, other, full, shots, traces, oy, oxz, inj,
    relay, load_sem, send_sem, recv_sem, relay_recv, relay_send, pair_sem, block_send, block_recv, shot_send, shot_recv, row_send, row_recv, ready, known,
):
    g = lax.axis_index("grid")
    s = lax.axis_index("shot")
    width, rows, depth = vt.shape
    half = depth // 2
    even = lax.rem(g, 2) == 0
    odd = lax.rem(g, 2) == 1
    has = (g > 0, g < n_grid - 1)
    near = (jnp.maximum(g - 1, 0), jnp.minimum(g + 1, n_grid - 1))
    place = lax.rem(g, 4)
    row = g // 4
    n_rows = n_grid // 4
    flipped = g + jnp.where(place < 2, 2, -2)

    def mate(k):
        return {"grid": jnp.where(lax.rem(k, 2) == lax.rem(s, 2), g, flipped), "shot": k}

    loads = [
        pltpu.make_async_copy(src, dst, load_sem.at[i])
        for i, (src, dst) in enumerate((
            (res_hbm, res),
            (enc_hbm, enc),
            (start_hbm.at[0], fb.at[pl.ds(4, width)]),
            (before_hbm.at[0], fa.at[pl.ds(4, width)]),
            (vt_hbm, vt),
            (cells_hbm, cells),
        ))
    ]
    for load in loads:
        load.start()

    barrier = pltpu.get_barrier_semaphore()

    def greet(**device):
        pl.semaphore_signal(barrier, inc=1, device_id=device, device_id_type=MESH)

    @pl.when(even)
    def _():
        greet(grid=near[1])

        @pl.when(has[0])
        def _():
            greet(grid=near[0])

        for i in range(1, n_shot):
            greet(**mate(lax.rem(s + i, n_shot)))
        for i in range(1, n_rows):
            greet(grid=lax.rem(g + 4 * i, n_grid))

    @pl.when(odd)
    def _():
        for i in range(n_rows):
            greet(grid=lax.rem(g - 1 + 4 * i, n_grid))

    zmat[...] = band_of(jnp.abs(iota((depth, depth), 0) - iota((depth, depth), 1)))
    ymat[...] = band_of(jnp.abs(iota((rows, 2 * rows), 0) - lax.rem(iota((rows, 2 * rows), 1), rows)))
    for f in (fa, fb):
        for p in (0, width + 4):
            f[pl.ds(p, 4)] = jnp.zeros((4, rows, depth), F32)

    def halo_copy(n, side, h, src):
        lanes = pl.ds(h * half, half)
        return pltpu.make_async_remote_copy(
            src_ref=stage.at[side] if (n, h) == (1, 0) else src.at[:, :, lanes],
            dst_ref=halo.at[n, 1 - side, :, :, lanes],
            send_sem=send_sem.at[n, side, h],
            recv_sem=recv_sem.at[n, 1 - side, h],
            device_id={"grid": near[side]},
            device_id_type=MESH,
        )

    def edge_of(n, side):
        if n == 0:
            return start_hbm.at[0, pl.ds(0 if side == 0 else width - 4, 4)]
        f = fb if n % 2 == 0 else fa
        return f.at[pl.ds(4 if side == 0 else width, 4)]

    strip = rows // n_rows
    by_relay = (row, n_rows - 1 - row)
    diagonal = (place == 0, place == 3)
    relay_at = (jnp.minimum(g + 2, n_grid - 1), jnp.maximum(g - 2, 0))

    def source_of(n, side, h, p):
        at = pl.ds(p * strip, strip)
        if (n, h) == (1, 0):
            return stage.at[side, :, at]
        return edge_of(n, side).at[:, at, pl.ds(h * half, half)]

    def direct_piece(n, side, h, p):
        return pltpu.make_async_remote_copy(
            src_ref=source_of(n, side, h, p),
            dst_ref=halo.at[n, 1 - side, :, pl.ds(p * strip, strip), pl.ds(h * half, half)],
            send_sem=send_sem.at[n, side, h],
            recv_sem=recv_sem.at[n, 1 - side, h],
            device_id={"grid": near[side]},
            device_id_type=MESH,
        )

    def relay_piece(n, side, h, p):
        return pltpu.make_async_remote_copy(
            src_ref=source_of(n, side, h, p),
            dst_ref=relay.at[n, h, p],
            send_sem=send_sem.at[n, side, h],
            recv_sem=relay_recv.at[n, h, p],
            device_id={"grid": relay_at[side]},
            device_id_type=MESH,
        )

    def onward_piece(n, side, h, p):
        target = jnp.maximum(g - 3, 0) if side == 0 else jnp.minimum(g + 3, n_grid - 1)
        return pltpu.make_async_remote_copy(
            src_ref=relay.at[n, h, p],
            dst_ref=halo.at[n, 1 - side, :, pl.ds(p * strip, strip), pl.ds(h * half, half)],
            send_sem=relay_send.at[n, h, p],
            recv_sem=recv_sem.at[n, 1 - side, h],
            device_id={"grid": target},
            device_id_type=MESH,
        )

    def each_onward(n, h, act):
        for side in (0, 1):
            @pl.when(place == 2 - side)
            def _():
                for p in range(n_rows - 1):
                    @pl.when(p < by_relay[side])
                    def _():
                        act(n, side, h, p)

    def forward(n, h):
        def act(n, side, h, p):
            relay_piece(n, side, h, p).wait_recv()
            onward_piece(n, side, h, p).start()

        each_onward(n, h, act)

    def send_direct(n, side, h):
        for p in range(n_rows):
            @pl.when(p >= by_relay[side])
            def _():
                direct_piece(n, side, h, p).start()

    def send_by_relay(n, side, h):
        for p in range(n_rows - 1):
            @pl.when(p < by_relay[side])
            def _():
                relay_piece(n, side, h, p).start()

    def send_halo(n, side, h):
        @pl.when(has[side] & jnp.logical_not(diagonal[side]))
        def _():
            halo_copy(n, side, h, edge_of(n, side)).start()

        @pl.when(has[side] & diagonal[side])
        def _():
            send_by_relay(n, side, h)
            send_direct(n, side, h)

    def wait_half_sent(n, side, h):
        @pl.when(has[side])
        def _():
            halo_copy(n, side, h, edge_of(n, side)).wait_send()

    def wait_sent(n):
        for side in (0, 1):
            for h in (1, 0):
                wait_half_sent(n, side, h)

    def pair_copy(target):
        return pltpu.make_async_remote_copy(
            src_ref=part, dst_ref=other, send_sem=pair_sem.at[0], recv_sem=pair_sem.at[1],
            device_id={"grid": target}, device_id_type=MESH,
        )

    def block_copy(y, sem, target):
        rows_of = full.at[:, pl.ds(8 * y, 8)]
        return pltpu.make_async_remote_copy(
            src_ref=rows_of, dst_ref=rows_of, send_sem=block_send.at[sem], recv_sem=block_recv.at[y],
            device_id={"grid": target}, device_id_type=MESH,
        )

    loads[0].wait()
    loads[1].wait()
    shot_rows, samples = res.shape[0] // 4, 4
    core = lax.rem(g, 2)
    r = iota((8 * n_shot, n_shot), 0)
    pick = jnp.where(r // 8 == iota((8 * n_shot, n_shot), 1), 1.0, 0.0).astype(BF16)
    spread = jnp.where(
        iota((shot_rows, 4 * shot_rows), 0) == iota((shot_rows, 4 * shot_rows), 1) // 4, 1.0, 0.0
    ).astype(BF16)
    weights = dot(dot(pick, enc[...]).astype(BF16), spread)
    wide = (8 * n_shot, 4 * shot_rows)
    weights = jnp.where(lax.rem(iota(wide, 0), 8) - 4 * core == lax.rem(iota(wide, 1), 4), weights, 0.0)
    part[...] = dot(weights.astype(BF16), res[...]).reshape(n_shot, 8, 128)

    @pl.when(odd)
    def _():
        pl.semaphore_wait(barrier, jnp.where(has[1], 2, 1))
        for side in (0, 1):
            @pl.when(has[side])
            def _():
                pl.semaphore_signal(ready.at[1 - side], inc=1, device_id={"grid": near[side]}, device_id_type=MESH)

    for side in (1, 0):
        @pl.when(even & has[side])
        def _():
            pl.semaphore_wait(ready.at[side], 1)
    @pl.when(place == 0)
    def _():
        pair_copy(near[1]).start()

    @pl.when(place == 3)
    def _():
        pair_copy(near[0]).start()

    @pl.when(place == 2)
    def _():
        pl.semaphore_signal(known, inc=1, device_id={"grid": near[1]}, device_id_type=MESH)

    over_y = (place == 2, place == 1)
    for side in (0, 1):
        @pl.when(jnp.logical_not(over_y[side] | ((place == 3) & (side == 1))))
        def _():
            send_halo(0, side, 1)

    @pl.when(place == 3)
    def _():
        @pl.when(has[1])
        def _():
            send_direct(0, 1, 1)

        pl.semaphore_wait(known, 1)

        @pl.when(has[1])
        def _():
            send_by_relay(0, 1, 1)

    @pl.when(place == 1)
    def _():
        pair_copy(near[0]).wait_recv()
        full[:, pl.ds(0, 8)] = part[...] + other[...]
        block_copy(0, 0, near[1]).start()
        block_copy(0, 1, near[0]).start()

    @pl.when(place == 2)
    def _():
        pair_copy(near[1]).wait_recv()
        full[:, pl.ds(8, 8)] = part[...] + other[...]
        block_copy(1, 0, near[0]).start()

    for side in (0, 1):
        @pl.when(over_y[side])
        def _():
            send_halo(0, side, 1)

    for load in loads[2:]:
        load.wait()

    def own_part(n, planes, lanes=pl.ds(0, depth)):
        cur, nxt = (fb, fa) if n % 2 == 0 else (fa, fb)

        def plane(x, carry):
            high, low = split(cur[x + 4])
            along = zmat[:, lanes]
            across = dot(jnp.concatenate([high, low], axis=1), jnp.concatenate([along, along], axis=0))
            at = slice(lanes.start, lanes.start + lanes.size)
            across = across + dot(ymat[...], jnp.concatenate([high[:, at], low[:, at]], axis=0))
            u = cur[x + 4, :, lanes]
            total = (3.0 * C0) * u + across * (1.0 / SCALE)
            for j, weight in enumerate((C1, C2, C3, C4), 1):
                total = total + weight * (cur[x + 4 + j, :, lanes] + cur[x + 4 - j, :, lanes])
            nxt[x + 4, :, lanes] = 2.0 * u - nxt[x + 4, :, lanes] + vt[x, :, lanes] * total
            return carry

        if planes is edges:
            lax.fori_loop(0, 4, plane, 0)
            lax.fori_loop(width - 4, width, plane, 0)
        else:
            lax.fori_loop(4, width - 4, plane, 0)

    def add_halo(n, side, h):
        nxt = fa if n % 2 == 0 else fb
        lanes = pl.ds(h * half, half)

        @pl.when(has[side])
        def _():
            halo_copy(n, 1 - side, h, edge_of(n, 1 - side)).wait_recv()
            if (n, h) == (1, 0):
                for p in range(4):
                    x = p - 4 if side == 0 else width + p
                    halo[n, side, p, :, lanes] = halo[n, side, p, :, lanes] + traces_at(0, x)
            layer = [halo[n, side, 4 - d if side == 0 else d - 1, :, lanes] for d in (1, 2, 3, 4)]
            for i in range(4):
                x = i if side == 0 else width - 1 - i
                total = C4 * layer[3 - i]
                for j, weight in ((1, C1), (2, C2), (3, C3)):
                    if j > i:
                        total = total + weight * layer[j - i - 1]
                value = nxt[x + 4, :, lanes] + vt[x, :, lanes] * total
                nxt[x + 4, :, lanes] = value
                if (n, h) == (0, 0):
                    stage[side, i if side == 0 else 3 - i] = value

    def traces_at(n, x):
        tile, lane = divmod(8 * (x + 8), half)
        values = inj[3 - n, :, pl.ds(tile * half, half)]
        moved = values if lane == 0 else pltpu.roll(values, half - lane, 1)
        return jnp.where(iota((rows, half), 1) < 8, moved, 0.0)

    def inject(n, planes):
        nxt = fa if n % 2 == 0 else fb
        for x in planes:
            nxt[x + 4, :, pl.ds(0, half)] = nxt[x + 4, :, pl.ds(0, half)] + traces_at(n, x)

    edges = list(range(4)) + list(range(width - 4, width))
    inner = list(range(4, width - 4))

    own_part(0, edges)
    for side in (0, 1):
        send_halo(0, side, 0)

    def shot_copy(k):
        return pltpu.make_async_remote_copy(
            src_ref=full.at[k], dst_ref=shots.at[s], send_sem=shot_send.at[k], recv_sem=shot_recv.at[s],
            device_id=mate(k), device_id_type=MESH,
        )

    def shot_arrival(k):
        return pltpu.make_async_remote_copy(
            src_ref=full.at[k], dst_ref=shots.at[k], send_sem=shot_send.at[k], recv_sem=shot_recv.at[k],
            device_id=mate(k), device_id_type=MESH,
        )

    def row_copy(i, core):
        return pltpu.make_async_remote_copy(
            src_ref=traces.at[row], dst_ref=traces.at[row], send_sem=row_send.at[i, core], recv_sem=row_recv.at[row],
            device_id={"grid": lax.rem(g + 4 * i + core, n_grid)}, device_id_type=MESH,
        )

    def row_arrival(i):
        return pltpu.make_async_remote_copy(
            src_ref=traces.at[i], dst_ref=traces.at[i], send_sem=row_send.at[0, 0], recv_sem=row_recv.at[i],
            device_id={"grid": near[0]}, device_id_type=MESH,
        )

    row_targets = [(i, core) for i in range(n_rows) for core in (0, 1) if i or core]

    @pl.when(place == 1)
    def _():
        block_copy(1, 2, near[1]).wait_recv()
        block_copy(1, 2, near[0]).start()

    @pl.when(place == 0)
    def _():
        block_copy(0, 0, near[1]).wait_recv()
        block_copy(1, 0, near[1]).wait_recv()

    @pl.when(place == 2)
    def _():
        block_copy(0, 0, near[0]).wait_recv()

    @pl.when(even)
    def _():
        shots[s] = full[s]
        pl.semaphore_wait(barrier, n_shot - 1 + 2 * n_rows - 1)
        for i in range(1, n_shot):
            shot_copy(lax.rem(s + i, n_shot)).start()

    n_rec = cells.shape[1]
    oy[...] = jnp.where(iota((rows, n_rec), 0) == cells[1:2, :], 1.0, 0.0).astype(BF16)
    spot = ((cells[0:1, :] - g * width + 8) * 8 + cells[2:3, :]).astype(F32)
    spot = jnp.transpose(jnp.broadcast_to(spot, (128, n_rec)))
    for tile in range(oxz.shape[1] // 128):
        lane = (iota((n_rec, 128), 1) + 128 * tile).astype(F32)
        oxz[:, pl.ds(128 * tile, 128)] = jnp.where(spot == lane, 1.0, 0.0).astype(BF16)

    forward(0, 1)
    for side in (0, 1):
        add_halo(0, side, 1)
        send_halo(1, side, 1)
    own_part(0, inner)
    forward(0, 0)

    for side in (0, 1):
        add_halo(0, side, 0)
        send_halo(1, side, 0)

    @pl.when(even)
    def _():
        for i in range(1, n_shot):
            shot_arrival(lax.rem(s + i, n_shot)).wait_recv()
        traces[row] = jnp.sum(shots[...], axis=0)
        for target in row_targets:
            row_copy(*target).start()

    own_part(1, edges, pl.ds(half, half))
    forward(1, 1)
    for side in (0, 1):
        add_halo(1, side, 1)
        send_halo(2, side, 1)
    own_part(1, inner, pl.ds(half, half))
    forward(1, 0)

    for i in range(n_rows):
        @pl.when(jnp.logical_not(even & (row == i)))
        def _():
            row_arrival(i).wait_recv()

    def build(t):
        values = jnp.concatenate([traces[i // 4, pl.ds(4 * (i % 4) + t, 1), :] for i in range(n_grid)], axis=1)
        scaled = [oy[...] * jnp.broadcast_to(piece, oy.shape) for piece in split(values)]
        total = dot(jnp.concatenate(scaled, axis=0), oxz[...])
        inj[t] = total[:rows] + total[rows:]

    build(3)
    build(2)
    inject(0, edges + inner)
    own_part(1, edges, pl.ds(0, half))
    inject(1, edges)
    for side in (0, 1):
        add_halo(1, side, 0)
        send_halo(2, side, 0)
    own_part(1, inner, pl.ds(0, half))
    inject(1, inner)
    build(1)
    build(0)

    for n in (2, 3):
        wait_sent(n - 1)
        own_part(n, edges)
        inject(n, edges)
        if n == 3:
            own_part(n, inner)
            inject(n, inner)
        for h in (1, 0):
            forward(n, h)
            for side in (0, 1):
                add_halo(n, side, h)
                if n < 3:
                    send_halo(n + 1, side, h)
            if h == 1 and n < 3:
                own_part(n, inner)
                inject(n, inner)

    wait_sent(0)
    for n in range(4):
        for h in (1, 0):
            each_onward(n, h, lambda *which: onward_piece(*which).wait_send())
    wait_sent(3)

    @pl.when(place == 0)
    def _():
        pair_copy(near[1]).wait_send()

    @pl.when(place == 3)
    def _():
        pair_copy(near[0]).wait_send()

    @pl.when(place == 1)
    def _():
        block_copy(0, 0, near[1]).wait_send()
        block_copy(0, 1, near[0]).wait_send()
        block_copy(1, 2, near[0]).wait_send()

    @pl.when(place == 2)
    def _():
        block_copy(1, 0, near[0]).wait_send()

    @pl.when(even)
    def _():
        for i in range(1, n_shot):
            shot_copy(lax.rem(s + i, n_shot)).wait_send()
        for target in row_targets:
            row_copy(*target).wait_send()


def local(n_grid, n_shot, residuals, encoding, receiver_cells, velocity_term, field_before, field_start):
    shot_rows, samples, local_receivers = residuals.shape
    width, rows, depth = velocity_term.shape
    flat = residuals.reshape(shot_rows * samples, local_receivers)
    n_rec = receiver_cells.shape[1]
    dma = pltpu.SemaphoreType.DMA
    padded = (width + 8, rows, depth)
    vmem = pl.BlockSpec(memory_space=pltpu.VMEM)
    hbm = [
        pltpu.with_memory_space_constraint(a, pltpu.HBM)
        for a in (flat, encoding, receiver_cells, velocity_term, field_before, field_start)
    ]
    fields = pl.pallas_call(
        functools.partial(kernel, n_grid, n_shot),
        out_shape=(pltpu.VMEM(padded, F32), pltpu.VMEM(padded, F32)),
        in_specs=[pl.BlockSpec(memory_space=pltpu.HBM)] * 6,
        out_specs=(vmem, vmem),
        scratch_shapes=[
            pltpu.VMEM((width, rows, depth), F32),
            pltpu.VMEM((4, 2, 4, rows, depth), F32),
            pltpu.VMEM((2, 4, rows, depth // 2), F32),
            pltpu.VMEM((depth, depth), BF16),
            pltpu.VMEM((rows, 2 * rows), BF16),
            pltpu.VMEM(flat.shape, BF16),
            pltpu.VMEM(encoding.shape, BF16),
            pltpu.VMEM(receiver_cells.shape, jnp.int32),
            pltpu.VMEM((n_shot, 8, local_receivers), F32),
            pltpu.VMEM((n_shot, 8, local_receivers), F32),
            pltpu.VMEM((n_shot, 16, local_receivers), F32),
            pltpu.VMEM((n_shot, 16, local_receivers), F32),
            pltpu.VMEM((n_grid // 4, 16, local_receivers), F32),
            pltpu.VMEM((rows, n_rec), BF16),
            pltpu.VMEM((n_rec, 8 * (width + 16)), BF16),
            pltpu.VMEM((4, rows, 8 * (width + 16)), F32),
            pltpu.VMEM((4, 2, n_grid // 4 - 1, 4, rows // (n_grid // 4), depth // 2), F32),
            dma((6,)),
            dma((4, 2, 2)),
            dma((4, 2, 2)),
            dma((4, 2, n_grid // 4 - 1)),
            dma((4, 2, n_grid // 4 - 1)),
            dma((2,)),
            dma((3,)),
            dma((2,)),
            dma((n_shot,)),
            dma((n_shot,)),
            dma((n_grid // 4, 2)),
            dma((n_grid // 4,)),
            pltpu.SemaphoreType.REGULAR((2,)),
            pltpu.SemaphoreType.REGULAR,
        ],
        compiler_params=pltpu.CompilerParams(
            collective_id=0, has_side_effects=True, vmem_limit_bytes=40 * 1024 * 1024
        ),
        name="window",
    )(*hbm)

    def flush(fa, fb, last, end, sem):
        copies = []
        for i, (field, out) in enumerate(((fa, last), (fb, end))):
            for j in range(4):
                size = width // 4
                copies.append(pltpu.make_async_copy(
                    field.at[pl.ds(4 + j * size, size)], out.at[0, pl.ds(j * size, size)], sem.at[i, j]
                ))
        for copy in copies:
            copy.start()
        for copy in copies:
            copy.wait()

    field = jax.ShapeDtypeStruct(field_start.shape, F32)
    return pl.pallas_call(
        flush,
        out_shape=(field, field),
        in_specs=[vmem, vmem],
        out_specs=[pl.BlockSpec(memory_space=pltpu.HBM)] * 2,
        scratch_shapes=[dma((2, 4))],
        compiler_params=pltpu.CompilerParams(vmem_limit_bytes=16 * 1024 * 1024),
        name="flush",
    )(*fields)


def solution(mesh):
    return jax.shard_map(
        functools.partial(local, mesh.shape["grid"], mesh.shape["shot"]),
        mesh=mesh,
        in_specs=(
            P("shot", None, "grid"),
            P(None, "shot"),
            P(),
            P("grid", None, None),
            P("shot", "grid", None, None),
            P("shot", "grid", None, None),
        ),
        out_specs=(P("shot", "grid", None, None), P("shot", "grid", None, None)),
        check_vma=False,
    )
```

```python
import functools

import jax
import jax.numpy as jnp
from jax import lax
from jax.experimental import pallas as pl
from jax.experimental.pallas import tpu as pltpu
from jax.sharding import PartitionSpec as P

C0, C1, C2, C3, C4 = (-205.0 / 72.0, 8.0 / 5.0, -1.0 / 5.0, 8.0 / 315.0, -1.0 / 560.0)
SCALE = 5040.0
BAND = (8064.0, -1008.0, 128.0, -9.0)
MESH = pl.DeviceIdType.MESH
F32 = jnp.float32
BF16 = jnp.bfloat16


def band_of(distance):
    value = jnp.zeros(distance.shape, F32)
    for j, weight in enumerate(BAND, 1):
        value = jnp.where(distance == j, weight, value)
    return value.astype(BF16)


def iota(shape, dim):
    return lax.broadcasted_iota(jnp.int32, shape, dim)


def split(value):
    high = value.astype(BF16)
    return high, (value - high.astype(F32)).astype(BF16)


def dot(a, b):
    return jnp.dot(a, b, preferred_element_type=F32)


def kernel(
    n_grid, n_shot, res_hbm, enc_hbm, cells_hbm, vt_hbm, before_hbm, start_hbm, fa, fb,
    vt, halo, stage, zmat, ymat, res, enc, cells, part, other, full, shots, traces, oy, oxz, inj,
    relay, load_sem, send_sem, recv_sem, relay_recv, relay_send, pair_sem, block_send, block_recv, shot_send, shot_recv, row_send, row_recv, ready, known,
):
    g = lax.axis_index("grid")
    s = lax.axis_index("shot")
    width, rows, depth = vt.shape
    half = depth // 2
    even = lax.rem(g, 2) == 0
    odd = lax.rem(g, 2) == 1
    has = (g > 0, g < n_grid - 1)
    near = (jnp.maximum(g - 1, 0), jnp.minimum(g + 1, n_grid - 1))
    place = lax.rem(g, 4)
    row = g // 4
    n_rows = n_grid // 4
    flipped = g + jnp.where(place < 2, 2, -2)

    def mate(k):
        return {"grid": jnp.where(lax.rem(k, 2) == lax.rem(s, 2), g, flipped), "shot": k}

    loads = [
        pltpu.make_async_copy(src, dst, load_sem.at[i])
        for i, (src, dst) in enumerate((
            (res_hbm, res),
            (enc_hbm, enc),
            (start_hbm.at[0], fb.at[pl.ds(4, width)]),
            (before_hbm.at[0], fa.at[pl.ds(4, width)]),
            (vt_hbm, vt),
            (cells_hbm, cells),
        ))
    ]
    for load in loads:
        load.start()

    barrier = pltpu.get_barrier_semaphore()

    def greet(**device):
        pl.semaphore_signal(barrier, inc=1, device_id=device, device_id_type=MESH)

    @pl.when(even)
    def _():
        greet(grid=near[1])

        @pl.when(has[0])
        def _():
            greet(grid=near[0])

        for i in range(1, n_shot):
            greet(**mate(lax.rem(s + i, n_shot)))
        for i in range(1, n_rows):
            greet(grid=lax.rem(g + 4 * i, n_grid))

    @pl.when(odd)
    def _():
        for i in range(n_rows):
            greet(grid=lax.rem(g - 1 + 4 * i, n_grid))

    zmat[...] = band_of(jnp.abs(iota((depth, depth), 0) - iota((depth, depth), 1)))
    ymat[...] = band_of(jnp.abs(iota((rows, 2 * rows), 0) - lax.rem(iota((rows, 2 * rows), 1), rows)))
    for f in (fa, fb):
        for p in (0, width + 4):
            f[pl.ds(p, 4)] = jnp.zeros((4, rows, depth), F32)

    def halo_copy(n, side, h, src):
        lanes = pl.ds(h * half, half)
        return pltpu.make_async_remote_copy(
            src_ref=stage.at[side] if (n, h) == (1, 0) else src.at[:, :, lanes],
            dst_ref=halo.at[n, 1 - side, :, :, lanes],
            send_sem=send_sem.at[n, side, h],
            recv_sem=recv_sem.at[n, 1 - side, h],
            device_id={"grid": near[side]},
            device_id_type=MESH,
        )

    def edge_of(n, side):
        if n == 0:
            return start_hbm.at[0, pl.ds(0 if side == 0 else width - 4, 4)]
        f = fb if n % 2 == 0 else fa
        return f.at[pl.ds(4 if side == 0 else width, 4)]

    strip = rows // n_rows
    by_relay = (row, n_rows - 1 - row)
    diagonal = (place == 0, place == 3)
    relay_at = (jnp.minimum(g + 2, n_grid - 1), jnp.maximum(g - 2, 0))

    def source_of(n, side, h, p):
        at = pl.ds(p * strip, strip)
        if (n, h) == (1, 0):
            return stage.at[side, :, at]
        return edge_of(n, side).at[:, at, pl.ds(h * half, half)]

    def direct_piece(n, side, h, p):
        return pltpu.make_async_remote_copy(
            src_ref=source_of(n, side, h, p),
            dst_ref=halo.at[n, 1 - side, :, pl.ds(p * strip, strip), pl.ds(h * half, half)],
            send_sem=send_sem.at[n, side, h],
            recv_sem=recv_sem.at[n, 1 - side, h],
            device_id={"grid": near[side]},
            device_id_type=MESH,
        )

    def relay_piece(n, side, h, p):
        return pltpu.make_async_remote_copy(
            src_ref=source_of(n, side, h, p),
            dst_ref=relay.at[n, h, p],
            send_sem=send_sem.at[n, side, h],
            recv_sem=relay_recv.at[n, h, p],
            device_id={"grid": relay_at[side]},
            device_id_type=MESH,
        )

    def onward_piece(n, side, h, p):
        target = jnp.maximum(g - 3, 0) if side == 0 else jnp.minimum(g + 3, n_grid - 1)
        return pltpu.make_async_remote_copy(
            src_ref=relay.at[n, h, p],
            dst_ref=halo.at[n, 1 - side, :, pl.ds(p * strip, strip), pl.ds(h * half, half)],
            send_sem=relay_send.at[n, h, p],
            recv_sem=recv_sem.at[n, 1 - side, h],
            device_id={"grid": target},
            device_id_type=MESH,
        )

    def each_onward(n, h, act):
        for side in (0, 1):
            @pl.when(place == 2 - side)
            def _():
                for p in range(n_rows - 1):
                    @pl.when(p < by_relay[side])
                    def _():
                        act(n, side, h, p)

    def forward(n, h):
        def act(n, side, h, p):
            relay_piece(n, side, h, p).wait_recv()
            onward_piece(n, side, h, p).start()

        each_onward(n, h, act)

    def send_direct(n, side, h):
        for p in range(n_rows):
            @pl.when(p >= by_relay[side])
            def _():
                direct_piece(n, side, h, p).start()

    def send_by_relay(n, side, h):
        for p in range(n_rows - 1):
            @pl.when(p < by_relay[side])
            def _():
                relay_piece(n, side, h, p).start()

    def send_halo(n, side, h):
        @pl.when(has[side] & jnp.logical_not(diagonal[side]))
        def _():
            halo_copy(n, side, h, edge_of(n, side)).start()

        @pl.when(has[side] & diagonal[side])
        def _():
            send_by_relay(n, side, h)
            send_direct(n, side, h)

    def wait_half_sent(n, side, h):
        @pl.when(has[side])
        def _():
            halo_copy(n, side, h, edge_of(n, side)).wait_send()

    def wait_sent(n):
        for side in (0, 1):
            for h in (1, 0):
                wait_half_sent(n, side, h)

    def pair_copy(target):
        return pltpu.make_async_remote_copy(
            src_ref=part, dst_ref=other, send_sem=pair_sem.at[0], recv_sem=pair_sem.at[1],
            device_id={"grid": target}, device_id_type=MESH,
        )

    def block_copy(y, sem, target):
        rows_of = full.at[:, pl.ds(8 * y, 8)]
        return pltpu.make_async_remote_copy(
            src_ref=rows_of, dst_ref=rows_of, send_sem=block_send.at[sem], recv_sem=block_recv.at[y],
            device_id={"grid": target}, device_id_type=MESH,
        )

    loads[0].wait()
    loads[1].wait()
    shot_rows, samples = res.shape[0] // 4, 4
    core = lax.rem(g, 2)
    r = iota((8 * n_shot, n_shot), 0)
    pick = jnp.where(r // 8 == iota((8 * n_shot, n_shot), 1), 1.0, 0.0).astype(BF16)
    spread = jnp.where(
        iota((shot_rows, 4 * shot_rows), 0) == iota((shot_rows, 4 * shot_rows), 1) // 4, 1.0, 0.0
    ).astype(BF16)
    weights = dot(dot(pick, enc[...]).astype(BF16), spread)
    wide = (8 * n_shot, 4 * shot_rows)
    weights = jnp.where(lax.rem(iota(wide, 0), 8) - 4 * core == lax.rem(iota(wide, 1), 4), weights, 0.0)
    part[...] = dot(weights.astype(BF16), res[...]).reshape(n_shot, 8, 128)

    @pl.when(odd)
    def _():
        pl.semaphore_wait(barrier, jnp.where(has[1], 2, 1))
        for side in (0, 1):
            @pl.when(has[side])
            def _():
                pl.semaphore_signal(ready.at[1 - side], inc=1, device_id={"grid": near[side]}, device_id_type=MESH)

    for side in (1, 0):
        @pl.when(even & has[side])
        def _():
            pl.semaphore_wait(ready.at[side], 1)
    @pl.when(place == 0)
    def _():
        pair_copy(near[1]).start()

    @pl.when(place == 3)
    def _():
        pair_copy(near[0]).start()

    @pl.when(place == 2)
    def _():
        pl.semaphore_signal(known, inc=1, device_id={"grid": near[1]}, device_id_type=MESH)

    over_y = (place == 2, place == 1)
    for side in (0, 1):
        @pl.when(jnp.logical_not(over_y[side] | ((place == 3) & (side == 1))))
        def _():
            send_halo(0, side, 1)

    @pl.when(place == 3)
    def _():
        @pl.when(has[1])
        def _():
            send_direct(0, 1, 1)

        pl.semaphore_wait(known, 1)

        @pl.when(has[1])
        def _():
            send_by_relay(0, 1, 1)

    @pl.when(place == 1)
    def _():
        pair_copy(near[0]).wait_recv()
        full[:, pl.ds(0, 8)] = part[...] + other[...]
        block_copy(0, 0, near[1]).start()
        block_copy(0, 1, near[0]).start()

    @pl.when(place == 2)
    def _():
        pair_copy(near[1]).wait_recv()
        full[:, pl.ds(8, 8)] = part[...] + other[...]
        block_copy(1, 0, near[0]).start()

    for side in (0, 1):
        @pl.when(over_y[side])
        def _():
            send_halo(0, side, 1)

    for load in loads[2:]:
        load.wait()

    def own_part(n, planes, lanes=pl.ds(0, depth)):
        cur, nxt = (fb, fa) if n % 2 == 0 else (fa, fb)

        def plane(x, carry):
            high, low = split(cur[x + 4])
            along = zmat[:, lanes]
            across = dot(jnp.concatenate([high, low], axis=1), jnp.concatenate([along, along], axis=0))
            at = slice(lanes.start, lanes.start + lanes.size)
            across = across + dot(ymat[...], jnp.concatenate([high[:, at], low[:, at]], axis=0))
            u = cur[x + 4, :, lanes]
            total = (3.0 * C0) * u + across * (1.0 / SCALE)
            for j, weight in enumerate((C1, C2, C3, C4), 1):
                total = total + weight * (cur[x + 4 + j, :, lanes] + cur[x + 4 - j, :, lanes])
            nxt[x + 4, :, lanes] = 2.0 * u - nxt[x + 4, :, lanes] + vt[x, :, lanes] * total
            return carry

        if planes is edges:
            lax.fori_loop(0, 4, plane, 0)
            lax.fori_loop(width - 4, width, plane, 0)
        else:
            lax.fori_loop(4, width - 4, plane, 0)

    def add_halo(n, side, h):
        nxt = fa if n % 2 == 0 else fb
        lanes = pl.ds(h * half, half)

        @pl.when(has[side])
        def _():
            halo_copy(n, 1 - side, h, edge_of(n, 1 - side)).wait_recv()
            if (n, h) == (1, 0):
                for p in range(4):
                    x = p - 4 if side == 0 else width + p
                    halo[n, side, p, :, lanes] = halo[n, side, p, :, lanes] + traces_at(0, x)
            layer = [halo[n, side, 4 - d if side == 0 else d - 1, :, lanes] for d in (1, 2, 3, 4)]
            for i in range(4):
                x = i if side == 0 else width - 1 - i
                total = C4 * layer[3 - i]
                for j, weight in ((1, C1), (2, C2), (3, C3)):
                    if j > i:
                        total = total + weight * layer[j - i - 1]
                value = nxt[x + 4, :, lanes] + vt[x, :, lanes] * total
                nxt[x + 4, :, lanes] = value
                if (n, h) == (0, 0):
                    stage[side, i if side == 0 else 3 - i] = value

    def traces_at(n, x):
        tile, lane = divmod(8 * (x + 8), half)
        values = inj[3 - n, :, pl.ds(tile * half, half)]
        moved = values if lane == 0 else pltpu.roll(values, half - lane, 1)
        return jnp.where(iota((rows, half), 1) < 8, moved, 0.0)

    def inject(n, planes):
        nxt = fa if n % 2 == 0 else fb
        for x in planes:
            nxt[x + 4, :, pl.ds(0, half)] = nxt[x + 4, :, pl.ds(0, half)] + traces_at(n, x)

    edges = list(range(4)) + list(range(width - 4, width))
    inner = list(range(4, width - 4))

    own_part(0, edges)
    for side in (0, 1):
        send_halo(0, side, 0)

    def shot_copy(k):
        return pltpu.make_async_remote_copy(
            src_ref=full.at[k], dst_ref=shots.at[s], send_sem=shot_send.at[k], recv_sem=shot_recv.at[s],
            device_id=mate(k), device_id_type=MESH,
        )

    def shot_arrival(k):
        return pltpu.make_async_remote_copy(
            src_ref=full.at[k], dst_ref=shots.at[k], send_sem=shot_send.at[k], recv_sem=shot_recv.at[k],
            device_id=mate(k), device_id_type=MESH,
        )

    def row_copy(i, core):
        return pltpu.make_async_remote_copy(
            src_ref=traces.at[row], dst_ref=traces.at[row], send_sem=row_send.at[i, core], recv_sem=row_recv.at[row],
            device_id={"grid": lax.rem(g + 4 * i + core, n_grid)}, device_id_type=MESH,
        )

    def row_arrival(i):
        return pltpu.make_async_remote_copy(
            src_ref=traces.at[i], dst_ref=traces.at[i], send_sem=row_send.at[0, 0], recv_sem=row_recv.at[i],
            device_id={"grid": near[0]}, device_id_type=MESH,
        )

    row_targets = [(i, core) for i in range(n_rows) for core in (0, 1) if i or core]

    @pl.when(place == 1)
    def _():
        block_copy(1, 2, near[1]).wait_recv()
        block_copy(1, 2, near[0]).start()

    @pl.when(place == 0)
    def _():
        block_copy(0, 0, near[1]).wait_recv()
        block_copy(1, 0, near[1]).wait_recv()

    @pl.when(place == 2)
    def _():
        block_copy(0, 0, near[0]).wait_recv()

    @pl.when(even)
    def _():
        shots[s] = full[s]
        pl.semaphore_wait(barrier, n_shot - 1 + 2 * n_rows - 1)
        for i in range(1, n_shot):
            shot_copy(lax.rem(s + i, n_shot)).start()

    n_rec = cells.shape[1]
    oy[...] = jnp.where(iota((rows, n_rec), 0) == cells[1:2, :], 1.0, 0.0).astype(BF16)
    spot = ((cells[0:1, :] - g * width + 8) * 8 + cells[2:3, :]).astype(F32)
    spot = jnp.transpose(jnp.broadcast_to(spot, (128, n_rec)))
    for tile in range(oxz.shape[1] // 128):
        lane = (iota((n_rec, 128), 1) + 128 * tile).astype(F32)
        oxz[:, pl.ds(128 * tile, 128)] = jnp.where(spot == lane, 1.0, 0.0).astype(BF16)

    forward(0, 1)
    for side in (0, 1):
        add_halo(0, side, 1)
        send_halo(1, side, 1)
    own_part(0, inner)
    forward(0, 0)

    for side in (0, 1):
        add_halo(0, side, 0)
        send_halo(1, side, 0)

    @pl.when(even)
    def _():
        for i in range(1, n_shot):
            shot_arrival(lax.rem(s + i, n_shot)).wait_recv()
        traces[row] = jnp.sum(shots[...], axis=0)
        for target in row_targets:
            row_copy(*target).start()

    own_part(1, edges, pl.ds(half, half))
    forward(1, 1)
    for side in (0, 1):
        add_halo(1, side, 1)
        send_halo(2, side, 1)
    own_part(1, inner, pl.ds(half, half))
    forward(1, 0)

    for i in range(n_rows):
        @pl.when(jnp.logical_not(even & (row == i)))
        def _():
            row_arrival(i).wait_recv()

    def build(t):
        values = jnp.concatenate([traces[i // 4, pl.ds(4 * (i % 4) + t, 1), :] for i in range(n_grid)], axis=1)
        scaled = [oy[...] * jnp.broadcast_to(piece, oy.shape) for piece in split(values)]
        total = dot(jnp.concatenate(scaled, axis=0), oxz[...])
        inj[t] = total[:rows] + total[rows:]

    build(3)
    build(2)
    inject(0, edges + inner)
    own_part(1, edges, pl.ds(0, half))
    inject(1, edges)
    for side in (0, 1):
        add_halo(1, side, 0)
        send_halo(2, side, 0)
    own_part(1, inner, pl.ds(0, half))
    inject(1, inner)

    for n in (2, 3):
        wait_sent(n - 1)
        own_part(n, edges)
        if n == 3:
            own_part(n, inner)
        for h in (1, 0):
            forward(n, h)
            for side in (0, 1):
                add_halo(n, side, h)
                if n < 3:
                    send_halo(n + 1, side, h)
            if h == 1:
                build(3 - n)
                inject(n, edges if n < 3 else edges + inner)
            if h == 1 and n < 3:
                own_part(n, inner)
                inject(n, inner)

    wait_sent(0)
    for n in range(4):
        for h in (1, 0):
            each_onward(n, h, lambda *which: onward_piece(*which).wait_send())
    wait_sent(3)

    @pl.when(place == 0)
    def _():
        pair_copy(near[1]).wait_send()

    @pl.when(place == 3)
    def _():
        pair_copy(near[0]).wait_send()

    @pl.when(place == 1)
    def _():
        block_copy(0, 0, near[1]).wait_send()
        block_copy(0, 1, near[0]).wait_send()
        block_copy(1, 2, near[0]).wait_send()

    @pl.when(place == 2)
    def _():
        block_copy(1, 0, near[0]).wait_send()

    @pl.when(even)
    def _():
        for i in range(1, n_shot):
            shot_copy(lax.rem(s + i, n_shot)).wait_send()
        for target in row_targets:
            row_copy(*target).wait_send()


def local(n_grid, n_shot, residuals, encoding, receiver_cells, velocity_term, field_before, field_start):
    shot_rows, samples, local_receivers = residuals.shape
    width, rows, depth = velocity_term.shape
    flat = residuals.reshape(shot_rows * samples, local_receivers)
    n_rec = receiver_cells.shape[1]
    dma = pltpu.SemaphoreType.DMA
    padded = (width + 8, rows, depth)
    vmem = pl.BlockSpec(memory_space=pltpu.VMEM)
    hbm = [
        pltpu.with_memory_space_constraint(a, pltpu.HBM)
        for a in (flat, encoding, receiver_cells, velocity_term, field_before, field_start)
    ]
    fields = pl.pallas_call(
        functools.partial(kernel, n_grid, n_shot),
        out_shape=(pltpu.VMEM(padded, F32), pltpu.VMEM(padded, F32)),
        in_specs=[pl.BlockSpec(memory_space=pltpu.HBM)] * 6,
        out_specs=(vmem, vmem),
        scratch_shapes=[
            pltpu.VMEM((width, rows, depth), F32),
            pltpu.VMEM((4, 2, 4, rows, depth), F32),
            pltpu.VMEM((2, 4, rows, depth // 2), F32),
            pltpu.VMEM((depth, depth), BF16),
            pltpu.VMEM((rows, 2 * rows), BF16),
            pltpu.VMEM(flat.shape, BF16),
            pltpu.VMEM(encoding.shape, BF16),
            pltpu.VMEM(receiver_cells.shape, jnp.int32),
            pltpu.VMEM((n_shot, 8, local_receivers), F32),
            pltpu.VMEM((n_shot, 8, local_receivers), F32),
            pltpu.VMEM((n_shot, 16, local_receivers), F32),
            pltpu.VMEM((n_shot, 16, local_receivers), F32),
            pltpu.VMEM((n_grid // 4, 16, local_receivers), F32),
            pltpu.VMEM((rows, n_rec), BF16),
            pltpu.VMEM((n_rec, 8 * (width + 16)), BF16),
            pltpu.VMEM((4, rows, 8 * (width + 16)), F32),
            pltpu.VMEM((4, 2, n_grid // 4 - 1, 4, rows // (n_grid // 4), depth // 2), F32),
            dma((6,)),
            dma((4, 2, 2)),
            dma((4, 2, 2)),
            dma((4, 2, n_grid // 4 - 1)),
            dma((4, 2, n_grid // 4 - 1)),
            dma((2,)),
            dma((3,)),
            dma((2,)),
            dma((n_shot,)),
            dma((n_shot,)),
            dma((n_grid // 4, 2)),
            dma((n_grid // 4,)),
            pltpu.SemaphoreType.REGULAR((2,)),
            pltpu.SemaphoreType.REGULAR,
        ],
        compiler_params=pltpu.CompilerParams(
            collective_id=0, has_side_effects=True, vmem_limit_bytes=40 * 1024 * 1024
        ),
        name="window",
    )(*hbm)

    def flush(fa, fb, last, end, sem):
        copies = []
        for i, (field, out) in enumerate(((fa, last), (fb, end))):
            for j in range(4):
                size = width // 4
                copies.append(pltpu.make_async_copy(
                    field.at[pl.ds(4 + j * size, size)], out.at[0, pl.ds(j * size, size)], sem.at[i, j]
                ))
        for copy in copies:
            copy.start()
        for copy in copies:
            copy.wait()

    field = jax.ShapeDtypeStruct(field_start.shape, F32)
    return pl.pallas_call(
        flush,
        out_shape=(field, field),
        in_specs=[vmem, vmem],
        out_specs=[pl.BlockSpec(memory_space=pltpu.HBM)] * 2,
        scratch_shapes=[dma((2, 4))],
        compiler_params=pltpu.CompilerParams(vmem_limit_bytes=16 * 1024 * 1024),
        name="flush",
    )(*fields)


def solution(mesh):
    return jax.shard_map(
        functools.partial(local, mesh.shape["grid"], mesh.shape["shot"]),
        mesh=mesh,
        in_specs=(
            P("shot", None, "grid"),
            P(None, "shot"),
            P(),
            P("grid", None, None),
            P("shot", "grid", None, None),
            P("shot", "grid", None, None),
        ),
        out_specs=(P("shot", "grid", None, None), P("shot", "grid", None, None)),
        check_vma=False,
    )
```
